512 devices in a mesh: kx: 16 (over z_hi, x), ky: 32 (over y, z_lo, core).
Axes of the slice: x: 4, y: 4, z: 16 (z_hi: 4, z_lo: 4; z = z_hi * 4 + z_lo), core: 2. Of those that a mesh axis runs over, the one named last changes fastest.
Arguments:
- states: bfloat16 [512, 4096, 128], P(('kx', 'ky')), may hold values from -6 to 6
- energies: bfloat16 [512, 128], P(('kx', 'ky')), may hold values from -2 to 2
- external: float32 [1, 4096], replicated, may hold values from -6 to 6
- reorder: int32 [2, 512, 4096], P(None, ('kx', 'ky')), may hold values from 0 to 4095, each once within a row
Outputs:
- band_response: float32 [512, 2, 1, 128, 128], P(('kx', 'ky'))
- density: float32 [2, 1, 4096], replicated
The draws below stay inside these ranges and needn't reach their ends.
Inputs may be any that keep to these rules, and one draw needn't show every extreme that they name: Each row reorder[q, k] is a permutation of the 4096 grid components.
All inputs are finite; a program needn't handle non-finite values.
Results may differ from the reference program's by a relative error of at most 0.0029.
Values may be sent and summed in bfloat16 or wider, within the bound.
No kernel may reach another device: no remote copies, remote signals or barrier semaphores. Data moves between devices by JAX's collectives and lax.ppermute only.
A program may use at most 64 MiB of HBM per device.

```python
import math
import jax
import jax.numpy as jnp
from jax import lax

GX = 64
GY = 64
NB = 128
NQ = 2
NDIR = 1
ITERS = 2
G = 4096
K = 512
N_KX = 16
N_KY = 32


def levels(own_key, shape, shards, smallest, largest):
    def one(dim, parts):
        steps = jax.random.uniform(jax.random.fold_in(jax.random.fold_in(own_key, 6), dim), (parts,), jnp.float32, smallest / len(shards), largest / len(shards))
        return jnp.repeat(jnp.exp(steps), shape[dim] // parts).reshape((-1,) + (1,) * (len(shape) - dim - 1))

    loudness = one(*shards[0])
    for cut in shards[1:]:
        loudness = loudness * one(*cut)
    return loudness


def noise(stream_key, extent, spread, bound, shards=(), kind=jnp.bfloat16):
    values = jax.random.normal(stream_key, extent, jnp.float32) * spread
    if len(shards) > 0:
        values = levels(stream_key, extent, shards, -0.22, 0.18) * values
    return jnp.clip(values, min=-bound, max=bound).astype(kind)


def setup_inputs(seed: int = 0) -> dict:
    splits = jax.random.split(jax.random.key(seed), 5)
    return {
        "states": noise(splits[0], (K, G, NB), 1.0, 6.0, ((0, 512),)),
        "energies": jnp.clip(jax.random.uniform(splits[1], (K, NB), jnp.float32, -2.0, 2.0) * levels(splits[1], (K, NB), ((0, 512),), -0.4, 0.0), -2.0, 2.0).astype(jnp.bfloat16),
        "external": noise(splits[2], (NDIR, G), 1.0, 6.0, (), jnp.float32),
        "reorder": jax.vmap(lambda own: jax.random.permutation(own, G))(jax.random.split(splits[3], NQ * K)).reshape((NQ, K, G)).astype(jnp.int32),
    }


SMEAR = 0.5
FERMI = 0.0
SCREEN = 4.0

def hartley_table(length):
    positions = jnp.arange(length, dtype=jnp.int32)
    phases = positions[:, None] * positions[None, :] % length
    angles = phases.astype(jnp.float32) * (2.0 * math.pi / length)
    return (jnp.cos(angles) + jnp.sin(angles)) / math.sqrt(length)

def screening(len_x, len_y):
    freq_x = jnp.arange(len_x, dtype=jnp.int32)
    freq_x = jnp.minimum(freq_x, len_x - freq_x).astype(jnp.float32)
    freq_y = jnp.arange(len_y, dtype=jnp.int32)
    freq_y = jnp.minimum(freq_y, len_y - freq_y).astype(jnp.float32)
    return 1.0 / (1.0 + (freq_x[:, None] ** 2 + freq_y[None, :] ** 2) / SCREEN)

def coulomb(density):
    fields = density.reshape(density.shape[:-1] + (GX, GY))
    table_x = hartley_table(GX)
    table_y = hartley_table(GY)
    spectra = jnp.einsum('pi,abij,jq->abpq', table_x, fields, table_y, precision=lax.Precision.HIGHEST)
    spectra = spectra * screening(GX, GY)
    result = jnp.einsum('pi,abij,jq->abpq', table_x, spectra, table_y, precision=lax.Precision.HIGHEST)
    return result.reshape(density.shape)

def occupation(energy):
    return 1.0 / (1.0 + jnp.exp((energy - FERMI) / SMEAR))

def respond(orbital, energy, far_states, far_energy, potential):
    orbital_wide = orbital.astype(jnp.float32)
    far_wide = far_states.astype(jnp.float32)
    energy = energy.astype(jnp.float32)
    far_energy = far_energy.astype(jnp.float32)
    weighted = (potential[:, :, None] * orbital_wide[None]).astype(jnp.bfloat16).astype(jnp.float32)
    band_mats = jnp.einsum('gm,agn->amn', far_wide, weighted, precision=lax.Precision.HIGHEST)
    band_mats = band_mats * (1.0 / math.sqrt(orbital.shape[0]))
    gap_matrix = far_energy[:, None] - energy[None, :]
    weight = (occupation(energy)[None, :] - occupation(far_energy)[:, None]) * gap_matrix / (gap_matrix * gap_matrix + SMEAR * SMEAR)
    response = weight[None] * band_mats
    response_low = response.astype(jnp.bfloat16).astype(jnp.float32)
    orbitals_out = jnp.einsum('gm,amn->agn', far_wide, response_low, precision=lax.Precision.HIGHEST)
    orbitals_out = orbitals_out * (1.0 / math.sqrt(orbital.shape[1]))
    contrib = lax.optimization_barrier(jnp.sum(orbital_wide[None] * orbitals_out, axis=2))
    return (response, contrib)

def reference(states, energies, external, reorder):
    potential = jnp.broadcast_to(external[None], (NQ, NDIR, G))

    def per_point(kpoint, potential):
        orbital = states[kpoint]
        energy = energies[kpoint]
        row_index = kpoint // N_KY
        col_index = kpoint % N_KY
        partners = [(row_index + 1) % N_KX * N_KY + col_index, row_index * N_KY + (col_index + 1) % N_KY]
        responses = []
        contribs = []
        for q_index in range(NQ):
            partner = partners[q_index]
            far_states = jnp.take(states[partner], reorder[q_index, kpoint], axis=0)
            response, contrib = respond(orbital, energy, far_states, energies[partner], potential[q_index])
            responses.append(response)
            contribs.append(contrib)
        return (jnp.stack(responses), jnp.stack(contribs))
    kpoints = jnp.arange(K, dtype=jnp.int32)
    for rounds in range(ITERS):
        band_response, contribs = lax.map(lambda kpoint: per_point(kpoint, potential), kpoints)
        density = lax.optimization_barrier(jnp.sum(contribs, axis=0)) * (1.0 / math.sqrt(K))
        if rounds + 1 < ITERS:
            potential = external[None] + coulomb(density)
    return (band_response, density)
```

```python
import math

import jax
import jax.numpy as jnp
from jax import lax
from jax.sharding import Mesh, PartitionSpec as P

AXES = ("zh", "x", "y", "zl", "core")
AXIS_SIZES = (4, 4, 4, 4, 2)
KX = ("zh", "x")
KY = ("y", "zl", "core")
PLANE = ("x", "y", "core")
COLUMN = ("zh", "zl")

GX = 64
GY = 64
NQ = 2
ITERS = 2


SMEAR = 0.5
FERMI = 0.0
SCREEN = 4.0


def passed_along(value, axis, steps):
    count = lax.axis_size(axis)
    pairs = [(source, (source + steps) % count) for source in range(count)]
    return lax.ppermute(value, axis, pairs)


def exchange(value, axes):
    return lax.all_to_all(value, axes, 0, 0, tiled=True)


def summed_everywhere(value):
    plane = lax.axis_size(PLANE)
    column = lax.axis_size(COLUMN)
    chunks = value.reshape(plane, -1, 128)
    part = jnp.sum(exchange(chunks, PLANE), axis=0)
    copies = jnp.broadcast_to(part[None], (column,) + part.shape)
    part = jnp.sum(exchange(copies, COLUMN), axis=0)
    copies = jnp.broadcast_to(part[None], (plane,) + part.shape)
    return exchange(copies, PLANE).reshape(value.shape)


def hartley_table(length):
    positions = jnp.arange(length, dtype=jnp.int32)
    phases = positions[:, None] * positions[None, :] % length
    angles = phases.astype(jnp.float32) * (2.0 * math.pi / length)
    return (jnp.cos(angles) + jnp.sin(angles)) / math.sqrt(length)


def screening(len_x, len_y):
    freq_x = jnp.arange(len_x, dtype=jnp.int32)
    freq_x = jnp.minimum(freq_x, len_x - freq_x).astype(jnp.float32)
    freq_y = jnp.arange(len_y, dtype=jnp.int32)
    freq_y = jnp.minimum(freq_y, len_y - freq_y).astype(jnp.float32)
    return 1.0 / (1.0 + (freq_x[:, None] ** 2 + freq_y[None, :] ** 2) / SCREEN)


def coulomb(density):
    fields = density.reshape(density.shape[:-1] + (GX, GY))
    table_x = hartley_table(GX)
    table_y = hartley_table(GY)
    spectra = jnp.einsum(
        "pi,abij,jq->abpq", table_x, fields, table_y, precision=lax.Precision.HIGHEST
    )
    spectra = spectra * screening(GX, GY)
    result = jnp.einsum(
        "pi,abij,jq->abpq", table_x, spectra, table_y, precision=lax.Precision.HIGHEST
    )
    return result.reshape(density.shape)


def occupation(energy):
    return 1.0 / (1.0 + jnp.exp((energy - FERMI) / SMEAR))


def respond(orbital, energy, far_states, far_energy, potential):
    energy = energy.astype(jnp.float32)
    far_energy = far_energy.astype(jnp.float32)
    weighted = (potential[:, :, None] * orbital[None].astype(jnp.float32)).astype(jnp.bfloat16)
    band_mats = jnp.einsum("gm,agn->amn", far_states, weighted, preferred_element_type=jnp.float32)
    band_mats = band_mats * (1.0 / math.sqrt(orbital.shape[0]))
    gap_matrix = far_energy[:, None] - energy[None, :]
    weight = (
        (occupation(energy)[None, :] - occupation(far_energy)[:, None])
        * gap_matrix
        / (gap_matrix * gap_matrix + SMEAR * SMEAR)
    )
    response = weight[None] * band_mats
    response_low = response.astype(jnp.bfloat16)
    orbitals_out = jnp.einsum(
        "gm,amn->agn", far_states, response_low, preferred_element_type=jnp.float32
    )
    orbitals_out = orbitals_out * (1.0 / math.sqrt(orbital.shape[1]))
    contrib = jnp.sum(orbital[None].astype(jnp.float32) * orbitals_out, axis=2)
    return (response, contrib)


def partner_of(q_index, orbital, energy, reorder):
    if q_index == 0:
        far_states, far_energy = passed_along((orbital, energy), KX, -1)
    else:
        far_states, far_energy = passed_along((orbital, energy), KY, -1)
    return (jnp.take(far_states, reorder[q_index, 0], axis=0), far_energy)


def shards(states, energies, external, reorder):
    orbital = states[0]
    energy = energies[0]
    kpoint_count = lax.axis_size(AXES)
    grid_size = orbital.shape[0]
    potential = jnp.broadcast_to(external[None], (NQ, external.shape[0], grid_size))
    fetched_all = [partner_of(q_index, orbital, energy, reorder) for q_index in range(NQ)]
    for rounds in range(ITERS):
        responses = []
        density_parts = []
        for q_index in range(NQ):
            far_states, far_energy = fetched_all[q_index]
            response, contrib = respond(orbital, energy, far_states, far_energy, potential[q_index])
            responses.append(response)
            density_parts.append(contrib)
        density = summed_everywhere(jnp.stack(density_parts))
        density = density * (1.0 / math.sqrt(kpoint_count))
        if rounds + 1 < ITERS:
            potential = external[None] + coulomb(density)
    return (jnp.stack(responses)[None], density)


def solution(mesh):
    fine = Mesh(mesh.devices.reshape(AXIS_SIZES), AXES)
    return jax.shard_map(
        shards,
        mesh=fine,
        in_specs=(
            P(AXES, None, None),
            P(AXES, None),
            P(),
            P(None, AXES, None),
        ),
        out_specs=(P(AXES, None, None, None, None), P()),
        check_vma=False,
    )
```

```python
import math

import jax
import jax.numpy as jnp
import numpy as np
from jax import lax
from jax.sharding import Mesh, PartitionSpec as P


AXES = ("zh", "x", "y", "zl", "core")
AXIS_SIZES = (4, 4, 4, 4, 2)
KX = ("zh", "x")
KY = ("y", "zl", "core")
PLANE = ("x", "y", "core")
COLUMN = ("zh", "zl")

GX = 64
GY = 64
NQ = 2
ITERS = 2


SMEAR = 0.5
FERMI = 0.0
SCREEN = 4.0


def passed_along(value, axis, steps):
    count = lax.axis_size(axis)
    pairs = [(source, (source + steps) % count) for source in range(count)]
    return lax.ppermute(value, axis, pairs)


def exchange(value, axes):
    return lax.all_to_all(value, axes, 0, 0, tiled=True)


def summed_everywhere(value):
    plane = lax.axis_size(PLANE)
    column = lax.axis_size(COLUMN)
    chunks = value.reshape(plane, -1, 128)
    part = jnp.sum(exchange(chunks, PLANE), axis=0)
    copies = jnp.broadcast_to(part[None], (column,) + part.shape)
    part = jnp.sum(exchange(copies, COLUMN), axis=0)
    copies = jnp.broadcast_to(part[None], (plane,) + part.shape)
    return exchange(copies, PLANE).reshape(value.shape)


def hartley_table(length):
    positions = np.arange(length)
    angles = positions[:, None] * positions[None, :] % length * (2.0 * math.pi / length)
    return ((np.cos(angles) + np.sin(angles)) / math.sqrt(length)).astype(np.float32)


def screening(len_x, len_y):
    freq_x = np.arange(len_x)
    freq_x = np.minimum(freq_x, len_x - freq_x)
    freq_y = np.arange(len_y)
    freq_y = np.minimum(freq_y, len_y - freq_y)
    return (1.0 / (1.0 + (freq_x[:, None] ** 2 + freq_y[None, :] ** 2) / SCREEN)).astype(np.float32)


def coulomb(density):
    fields = density.reshape(density.shape[:-1] + (GX, GY))
    table_x = hartley_table(GX)
    table_y = hartley_table(GY)
    spectra = jnp.einsum(
        "pi,abij,jq->abpq", table_x, fields, table_y, precision=lax.Precision.HIGHEST
    )
    spectra = spectra * screening(GX, GY)
    result = jnp.einsum(
        "pi,abij,jq->abpq", table_x, spectra, table_y, precision=lax.Precision.HIGHEST
    )
    return result.reshape(density.shape)


def occupation(energy):
    return 1.0 / (1.0 + jnp.exp((energy - FERMI) / SMEAR))


def respond(orbital, energy, far_states, far_energy, potential):
    energy = energy.astype(jnp.float32)
    far_energy = far_energy.astype(jnp.float32)
    weighted = (potential[:, :, None] * orbital[None].astype(jnp.float32)).astype(jnp.bfloat16)
    band_mats = jnp.einsum("gm,agn->amn", far_states, weighted, preferred_element_type=jnp.float32)
    band_mats = band_mats * (1.0 / math.sqrt(orbital.shape[0]))
    gap_matrix = far_energy[:, None] - energy[None, :]
    weight = (
        (occupation(energy)[None, :] - occupation(far_energy)[:, None])
        * gap_matrix
        / (gap_matrix * gap_matrix + SMEAR * SMEAR)
    )
    response = weight[None] * band_mats
    response_low = response.astype(jnp.bfloat16)
    orbitals_out = jnp.einsum(
        "gm,amn->agn", far_states, response_low, preferred_element_type=jnp.float32
    )
    orbitals_out = orbitals_out * (1.0 / math.sqrt(orbital.shape[1]))
    contrib = jnp.sum(orbital[None].astype(jnp.float32) * orbitals_out, axis=2)
    return (response, contrib)


def spread_along_x(orbital):
    rows = orbital.shape[0]
    outer = rows * 5 // 16
    inner = rows // 2 - outer
    cuts = (0, outer, outer + inner, outer + 2 * inner, rows)
    parts = [orbital[cuts[c] : cuts[c + 1]] for c in range(4)]
    orbital, parts = lax.optimization_barrier((orbital, parts))
    column = lax.axis_index("x")
    spread = [lax.ppermute(parts[c], "x", [(0, c)]) for c in range(1, 4)]
    wide = jnp.where(column == 0, parts[0], spread[2])
    narrow = jnp.where(column == 1, spread[0], spread[1])
    count = lax.axis_size("zh")
    hops = [(source, (source - 1) % count) for source in range(count)]
    wide = lax.ppermute(wide, KX, [(4 * s + x, 4 * t + x) for s, t in hops for x in (0, 3)])
    narrow = lax.ppermute(narrow, KX, [(4 * s + x, 4 * t + x) for s, t in hops for x in (1, 2)])
    return (orbital, wide, narrow)


def collected_along_x(wide, narrow):
    first = lax.ppermute(wide, "x", [(0, 3)])
    middle = [lax.ppermute(narrow, "x", [(x, 3)]) for x in (1, 2)]
    return jnp.concatenate([first] + middle + [wide])


def shards(states, energies, external, reorder):
    orbital = states[0]
    energy = energies[0]
    kpoint_count = lax.axis_size(AXES)
    grid_size = orbital.shape[0]
    potential = jnp.broadcast_to(external[None], (NQ, external.shape[0], grid_size))
    sent, wide, narrow = spread_along_x(orbital)
    beside = lax.ppermute(sent, "x", [(1, 0), (2, 1), (3, 2)])
    second_states = passed_along(sent, KY, -1)
    second_states, own_energy = lax.optimization_barrier((second_states, energy))
    second_energy = passed_along(own_energy, KY, -1)
    first_energy = passed_along(own_energy, KX, -1)
    second_states = jnp.take(second_states, reorder[1, 0], axis=0)
    second = respond(orbital, energy, second_states, second_energy, potential[1])
    second, wide, narrow, beside = lax.optimization_barrier((second, wide, narrow, beside))
    wrapped = collected_along_x(wide, narrow)
    first_states = jnp.where(lax.axis_index("x") == 3, wrapped, beside)
    first_states = jnp.take(first_states, reorder[0, 0], axis=0)
    first = respond(orbital, energy, first_states, first_energy, potential[0])
    for rounds in range(ITERS):
        if rounds > 0:
            first = respond(orbital, energy, first_states, first_energy, potential[0])
            second = respond(orbital, energy, second_states, second_energy, potential[1])
        density = summed_everywhere(jnp.stack([first[1], second[1]]))
        density = density * (1.0 / math.sqrt(kpoint_count))
        if rounds + 1 < ITERS:
            potential = external[None] + coulomb(density)
    return (jnp.stack([first[0], second[0]])[None], density)


def solution(mesh):
    fine = Mesh(mesh.devices.reshape(AXIS_SIZES), AXES)
    return jax.shard_map(
        shards,
        mesh=fine,
        in_specs=(
            P(AXES, None, None),
            P(AXES, None),
            P(),
            P(None, AXES, None),
        ),
        out_specs=(P(AXES, None, None, None, None), P()),
        check_vma=False,
    )
```

```python
import math

import jax
import jax.numpy as jnp
import numpy as np
from jax import lax
from jax.experimental import pallas as pl
from jax.experimental.pallas import tpu as pltpu
from jax.sharding import Mesh, PartitionSpec as P


AXES = ("zh", "x", "y", "zl", "core")
AXIS_SIZES = (4, 4, 4, 4, 2)
KX = ("zh", "x")
KY = ("y", "zl", "core")
PLANE = ("x", "y", "core")
COLUMN = ("zh", "zl")

GX = 64
GY = 64
NQ = 2
GRID = GX * GY
BANDS = 128
LANES = 128
ROWS = GRID // LANES
STEP = 512

SMEAR = 0.5
FERMI = 0.0
SCREEN = 4.0


def hartley_table(length):
    positions = np.arange(length)
    angles = positions[:, None] * positions[None, :] % length * (2.0 * math.pi / length)
    return (np.cos(angles) + np.sin(angles)) / math.sqrt(length)


def screening(len_x, len_y):
    freq_x = np.arange(len_x)
    freq_x = np.minimum(freq_x, len_x - freq_x)
    freq_y = np.arange(len_y)
    freq_y = np.minimum(freq_y, len_y - freq_y)
    return 1.0 / (1.0 + (freq_x[:, None] ** 2 + freq_y[None, :] ** 2) / SCREEN)


def lane_block(index):
    return pl.ds(pl.multiple_of(index * LANES, LANES), LANES)


def in_parts(value):
    high = value.astype(jnp.bfloat16)
    rest = value - high.astype(jnp.float32)
    middle = rest.astype(jnp.bfloat16)
    low = (rest - middle.astype(jnp.float32)).astype(jnp.bfloat16)
    return (high, middle, low)


def occupation(energy):
    return 1.0 / (1.0 + jnp.exp((energy - FERMI) / SMEAR))


def across(row):
    return jnp.broadcast_to(row, (BANDS, BANDS)).T


def weights(energy, far_energy):
    energy = energy.astype(jnp.float32)
    far_energy = far_energy.astype(jnp.float32)
    gap = far_energy - across(energy)
    filled = across(occupation(energy)) - occupation(far_energy)
    return filled * gap / (gap * gap + SMEAR * SMEAR)


def weigh(potential_ref, own_ref, weighted_ref):
    for block in range(ROWS):
        at = slice(block * LANES, (block + 1) * LANES)
        product = potential_ref[block : block + 1, :] * own_ref[:, at].astype(jnp.float32)
        weighted_ref[:, at] = product.astype(jnp.bfloat16)


def respond(weighted_ref, far_ref, own_ref, weight, terms_ref):
    bands = jnp.zeros((BANDS, BANDS), jnp.float32)
    for start in range(0, GRID, STEP):
        at = slice(start, start + STEP)
        bands += jnp.dot(weighted_ref[:, at], far_ref[at, :], preferred_element_type=jnp.float32)
    response = weight * (bands * (1.0 / math.sqrt(GRID)))
    low = response.astype(jnp.bfloat16)
    for start in range(0, GRID, STEP):
        at = slice(start, start + STEP)
        orbitals = lax.dot_general(
            low, far_ref[at, :], (((1,), (1,)), ((), ())), preferred_element_type=jnp.float32
        )
        term = jnp.sum(own_ref[:, at].astype(jnp.float32) * orbitals, axis=0, keepdims=True)
        term = term * (1.0 / math.sqrt(BANDS))
        for block in range(STEP // LANES):
            row = start // LANES + block
            terms_ref[row : row + 1, :] = term[:, block * LANES : (block + 1) * LANES]
    return response


def to_far_order(value_ref, order_ref, column_ref, parts_ref):
    parts = in_parts(value_ref[...])
    rows = lax.broadcasted_iota(jnp.int32, (ROWS, LANES), 0)
    for block in range(ROWS):
        mine = (order_ref[block : block + 1, :] // LANES) == rows
        at = slice(block * LANES, (block + 1) * LANES)
        for index, part in enumerate(parts):
            wide = part[block : block + 1, :].astype(jnp.float32)
            parts_ref[index * ROWS : (index + 1) * ROWS, at] = jnp.where(mine, wide, 0.0).astype(jnp.bfloat16)
    sums = lax.dot_general(
        parts_ref[...], column_ref[...], (((1,), (1,)), ((), ())), preferred_element_type=jnp.float32
    )
    return sums[:ROWS] + sums[ROWS : 2 * ROWS] + sums[2 * ROWS :]


def from_far_order(value, order_ref, column_ref, out_ref, first_row):
    stacked = jnp.concatenate([part.astype(jnp.float32) for part in in_parts(value)]).astype(jnp.bfloat16)
    rows = lax.broadcasted_iota(jnp.int32, (ROWS, LANES), 0)
    for start in range(0, GRID, STEP):
        at = slice(start, start + STEP)
        spread = jnp.dot(stacked, column_ref[:, at], preferred_element_type=jnp.float32)
        spread = spread[:ROWS] + spread[ROWS : 2 * ROWS] + spread[2 * ROWS :]
        for block in range(STEP // LANES):
            row = start // LANES + block
            mine = (order_ref[row : row + 1, :] // LANES) == rows
            picked = jnp.where(mine, spread[:, block * LANES : (block + 1) * LANES], 0.0)
            out_ref[first_row + row : first_row + row + 1, :] = jnp.sum(picked, axis=0, keepdims=True)


UNROLL = 32


def prepare_kernel(order_smem, own_ref, order_ref, external_ref,
                   turned_ref, moved_ref, weighted_ref, column_ref, wide, scattered, parts, potential):
    wide[...] = own_ref[...].astype(jnp.float32)

    def move(step, carry):
        base = step * UNROLL
        for offset in range(UNROLL):
            row = base + offset
            scattered[pl.ds(order_smem[row], 1), :] = wide[pl.ds(row, 1), :]
        return carry

    lax.fori_loop(0, GRID // UNROLL, move, 0)
    columns = lax.broadcasted_iota(jnp.int32, (LANES, LANES), 0)

    def turn(block, carry):
        at = lane_block(block)
        turned_ref[:, at] = wide[at, :].T.astype(jnp.bfloat16)
        moved_ref[:, at] = scattered[at, :].T.astype(jnp.bfloat16)
        mine = (order_ref[pl.ds(block, 1), :] % LANES) == columns
        column_ref[:, at] = jnp.where(mine, 1.0, 0.0).astype(jnp.bfloat16)
        return carry

    lax.fori_loop(0, ROWS, turn, 0)
    potential[...] = to_far_order(external_ref, order_ref, column_ref, parts)
    weigh(potential, moved_ref, weighted_ref)


def second_kernel(order_smem, sent_ref, turned_ref, external_ref, energy_ref, far_energy_ref,
                  far_ref, terms_ref, wide, gathered, weighted):
    wide[...] = sent_ref[...].astype(jnp.float32)

    def move(step, carry):
        base = step * UNROLL
        for offset in range(UNROLL):
            row = base + offset
            gathered[pl.ds(row, 1), :] = wide[pl.ds(order_smem[row], 1), :]
        return carry

    lax.fori_loop(0, GRID // UNROLL, move, 0)
    far_ref[...] = gathered[...].astype(jnp.bfloat16)
    weigh(external_ref, turned_ref, weighted)
    respond(weighted, far_ref, turned_ref, weights(energy_ref[...], far_energy_ref[...]), terms_ref)


def first_kernel(flag_smem, *refs):
    piece_refs = refs[:4]
    (beside_ref, moved_ref, weighted_ref, order_ref, column_ref, energy_ref, far_energy_ref, other_ref,
     far_ref, terms_ref, own_terms) = refs[4:]

    @pl.when(flag_smem[0] == 1)
    def _():
        start = 0
        for piece in piece_refs:
            far_ref[start : start + piece.shape[0], :] = piece[...]
            start += piece.shape[0]

    @pl.when(flag_smem[0] == 0)
    def _():
        far_ref[...] = beside_ref[...]

    respond(weighted_ref, far_ref, moved_ref, weights(energy_ref[...], far_energy_ref[...]), own_terms)
    from_far_order(own_terms[...], order_ref, column_ref, terms_ref, 0)
    terms_ref[ROWS:, :] = other_ref[...]


def exact_dot(left, right):
    return jnp.dot(left, right, precision=lax.Precision.HIGHEST, preferred_element_type=jnp.float32)


def last_kernel(density_ref, external_ref, even_ref, odd_ref, into_ref, back_ref, screen_ref, even_t_ref, odd_t_ref,
                first_ref, second_ref, moved_ref, turned_ref, order_ref, column_ref,
                energy_ref, first_energy_ref, second_energy_ref,
                response_ref, terms_ref, parts, potential, moved_potential, weighted, own_terms):
    scale = 1.0 / math.sqrt(math.prod(AXIS_SIZES))
    low_half = lax.broadcasted_iota(jnp.int32, (ROWS, LANES), 1) < GY
    along_y = exact_dot(density_ref[...] * scale, into_ref[...])
    for q_index in range(NQ):
        at = slice(q_index * ROWS, (q_index + 1) * ROWS)
        spectrum = exact_dot(even_ref[...], along_y[at, :LANES]) + exact_dot(odd_ref[...], along_y[at, LANES:])
        back = exact_dot(spectrum * screen_ref[...], back_ref[...])
        field = jnp.where(low_half, exact_dot(even_t_ref[...], back), exact_dot(odd_t_ref[...], back))
        potential[at, :] = external_ref[...] + field
    moved_potential[...] = to_far_order(potential.at[0:ROWS], order_ref, column_ref, parts)
    weigh(moved_potential, moved_ref, weighted)
    weight = weights(energy_ref[...], first_energy_ref[...])
    response_ref[0] = respond(weighted, first_ref, moved_ref, weight, own_terms).T
    from_far_order(own_terms[...], order_ref, column_ref, terms_ref, 0)
    weigh(potential.at[ROWS : 2 * ROWS], turned_ref, weighted)
    weight = weights(energy_ref[...], second_energy_ref[...])
    response_ref[1] = respond(weighted, second_ref, turned_ref, weight, own_terms).T
    terms_ref[ROWS:, :] = own_terms[...]


def coulomb_tables():
    table = hartley_table(GX)
    other = hartley_table(GY)
    none = np.zeros((GY, 2 * GY))
    twice = np.concatenate([other, other], axis=1)
    into = np.concatenate([np.concatenate([twice, none]), np.concatenate([none, twice])], axis=1)
    back = np.concatenate([twice, none])
    screen = screening(GX, GY)
    screen = np.concatenate([screen, screen], axis=1)
    even, odd = table[:, 0::2], table[:, 1::2]
    return [part.astype(np.float32) for part in (even, odd, into, back, screen, even.T, odd.T)]


VMEM = pl.BlockSpec(memory_space=pltpu.VMEM)
SMEM = pl.BlockSpec(memory_space=pltpu.SMEM)


def local_call(kernel, smem, arrays, outs, scratch, microseconds):
    return pl.pallas_call(
        kernel,
        out_shape=[jax.ShapeDtypeStruct(shape, kind) for shape, kind in outs],
        in_specs=[SMEM] * smem + [VMEM] * (len(arrays) - smem),
        out_specs=[VMEM] * len(outs),
        scratch_shapes=[pltpu.VMEM(shape, kind) for shape, kind in scratch],
        cost_estimate=pl.CostEstimate(flops=0, bytes_accessed=microseconds * 3000000, transcendentals=0),
    )(*arrays)


F32 = jnp.float32
BF16 = jnp.bfloat16
TALL = (GRID, BANDS)
TURNED = (BANDS, GRID)
BLOCKS = (ROWS, LANES)


def prepare(order, own, order_blocks, external):
    return local_call(
        prepare_kernel, 1, (order, own, order_blocks, external),
        [(TURNED, BF16)] * 3 + [((LANES, GRID), BF16)],
        [(TALL, F32), (TALL, F32), ((3 * ROWS, GRID), BF16), (BLOCKS, F32)], 12,
    )


def second_round_one(order, sent, turned, external, energy, far_energy):
    return local_call(
        second_kernel, 1, (order, sent, turned, external, energy, far_energy),
        [(TALL, BF16), (BLOCKS, F32)], [(TALL, F32), (TALL, F32), (TURNED, BF16)], 12,
    )


def first_round_one(flag, pieces, beside, moved, weighted, order_blocks, column, energy, far_energy, other):
    arrays = (flag, *pieces, beside, moved, weighted, order_blocks, column, energy, far_energy, other)
    return local_call(first_kernel, 1, arrays, [(TALL, BF16), ((2 * ROWS, LANES), F32)], [(BLOCKS, F32)], 3)


def round_two(density, external, first, second, moved, turned, order_blocks, column, energy, first_energy, second_energy):
    arrays = (density, external, *[jnp.asarray(part) for part in coulomb_tables()], first, second, moved, turned,
              order_blocks, column, energy, first_energy, second_energy)
    return local_call(
        last_kernel, 0, arrays,
        [((NQ, BANDS, BANDS), F32), ((2 * ROWS, LANES), F32)],
        [((3 * ROWS, GRID), BF16), ((2 * ROWS, LANES), F32), (BLOCKS, F32), (TURNED, BF16), (BLOCKS, F32)], 5,
    )


def exchange(value, axes):
    return lax.all_to_all(value, axes, 0, 0, tiled=True)


def summed_everywhere(value):
    plane = lax.axis_size(PLANE)
    column = lax.axis_size(COLUMN)
    chunks = value.reshape(plane, -1, LANES)
    part = jnp.sum(exchange(chunks, PLANE), axis=0)
    copies = jnp.broadcast_to(part[None], (column,) + part.shape)
    part = jnp.sum(exchange(copies, COLUMN), axis=0)
    copies = jnp.broadcast_to(part[None], (plane,) + part.shape)
    return exchange(copies, PLANE).reshape(value.shape)


def next_along(value, axis):
    count = lax.axis_size(axis)
    return lax.ppermute(value, axis, [(source, (source - 1) % count) for source in range(count)])


def iterate(states, energies, external, reorder):
    orbital = states[0]
    external = external.reshape(BLOCKS)
    order_blocks = reorder[0, 0].reshape(BLOCKS)
    column_index = lax.axis_index("x")

    outer = GRID * 5 // 16
    inner = GRID // 2 - outer
    cuts = (0, outer, outer + inner, outer + 2 * inner, GRID)
    parts = [orbital[cuts[c] : cuts[c + 1]] for c in range(4)]
    spread = [lax.ppermute(parts[c], "x", [(0, c)]) for c in range(1, 4)]
    far_second = next_along(orbital, KY)
    beside = lax.ppermute(orbital, "x", [(1, 0), (2, 1), (3, 2)])
    wide = jnp.where(column_index == 0, parts[0], spread[2])
    narrow = jnp.where(column_index == 1, spread[0], spread[1])
    wide, narrow, own = lax.optimization_barrier((wide, narrow, orbital))
    count = lax.axis_size("zh")
    hops = [(source, (source - 1) % count) for source in range(count)]
    wide = lax.ppermute(wide, KX, [(4 * s + x, 4 * t + x) for s, t in hops for x in (0, 3)])
    narrow = lax.ppermute(narrow, KX, [(4 * s + x, 4 * t + x) for s, t in hops for x in (1, 2)])
    second_energy = next_along(energies, KY)
    first_energy = next_along(energies, KX)

    turned, moved, weighted, column = prepare(reorder[0, 0], own, order_blocks, external)
    second_states, second_terms = second_round_one(
        reorder[1, 0], far_second, turned, external, energies, second_energy
    )

    second_terms, wide, narrow = lax.optimization_barrier((second_terms, wide, narrow))
    pieces = [lax.ppermute(wide, "x", [(0, 3)])]
    pieces += [lax.ppermute(narrow, "x", [(x, 3)]) for x in (1, 2)]
    flag = (column_index == 3).astype(jnp.int32).reshape(1)
    first_states, terms = first_round_one(
        flag, pieces + [wide], beside, moved, weighted, order_blocks, column, energies, first_energy, second_terms
    )
    response, terms = round_two(
        summed_everywhere(terms), external, first_states, second_states, moved, turned, order_blocks, column,
        energies, first_energy, second_energy,
    )
    density = summed_everywhere(terms) * (1.0 / math.sqrt(lax.axis_size(AXES)))
    return (response.reshape(1, NQ, 1, BANDS, BANDS), density.reshape(NQ, 1, GRID))


def solution(mesh):
    fine = Mesh(mesh.devices.reshape(AXIS_SIZES), AXES)
    return jax.shard_map(
        iterate,
        mesh=fine,
        in_specs=(
            P(AXES, None, None),
            P(AXES, None),
            P(),
            P(None, AXES, None),
        ),
        out_specs=(P(AXES, None, None, None, None), P()),
        check_vma=False,
    )
```

```python
import math

import jax
import jax.numpy as jnp
import numpy as np
from jax import lax
from jax.experimental import pallas as pl
from jax.experimental.pallas import tpu as pltpu
from jax.sharding import Mesh, PartitionSpec as P


AXES = ("zh", "x", "y", "zl", "core")
AXIS_SIZES = (4, 4, 4, 4, 2)
KX = ("zh", "x")
KY = ("y", "zl", "core")
PLANE = ("x", "y", "core")
COLUMN = ("zh", "zl")

GX = 64
GY = 64
NQ = 2
GRID = GX * GY
BANDS = 128
LANES = 128
ROWS = GRID // LANES
STEP = 512
LIMIT = 24 * 1024 * 1024

SMEAR = 0.5
FERMI = 0.0
SCREEN = 4.0


def hartley_table(length):
    positions = np.arange(length)
    angles = positions[:, None] * positions[None, :] % length * (2.0 * math.pi / length)
    return (np.cos(angles) + np.sin(angles)) / math.sqrt(length)


def screening(len_x, len_y):
    freq_x = np.arange(len_x)
    freq_x = np.minimum(freq_x, len_x - freq_x)
    freq_y = np.arange(len_y)
    freq_y = np.minimum(freq_y, len_y - freq_y)
    return 1.0 / (1.0 + (freq_x[:, None] ** 2 + freq_y[None, :] ** 2) / SCREEN)


def lane_block(index):
    return pl.ds(pl.multiple_of(index * LANES, LANES), LANES)


def in_parts(value):
    high = value.astype(jnp.bfloat16)
    rest = value - high.astype(jnp.float32)
    middle = rest.astype(jnp.bfloat16)
    low = (rest - middle.astype(jnp.float32)).astype(jnp.bfloat16)
    return (high, middle, low)


def occupation(energy):
    return 1.0 / (1.0 + jnp.exp((energy - FERMI) / SMEAR))


def across(row):
    return jnp.broadcast_to(row, (BANDS, BANDS)).T


def weights(energy, far_energy):
    energy = energy.astype(jnp.float32)
    far_energy = far_energy.astype(jnp.float32)
    gap = far_energy - across(energy)
    filled = across(occupation(energy)) - occupation(far_energy)
    return filled * gap / (gap * gap + SMEAR * SMEAR)


def weigh(potential_ref, own_ref, weighted_ref):
    for block in range(ROWS):
        at = slice(block * LANES, (block + 1) * LANES)
        product = potential_ref[block : block + 1, :] * own_ref[:, at].astype(jnp.float32)
        weighted_ref[:, at] = product.astype(jnp.bfloat16)


def respond(weighted_ref, far_ref, own_ref, weight, terms_ref):
    bands = jnp.zeros((BANDS, BANDS), jnp.float32)
    for start in range(0, GRID, STEP):
        at = slice(start, start + STEP)
        bands += jnp.dot(weighted_ref[:, at], far_ref[at, :], preferred_element_type=jnp.float32)
    response = weight * (bands * (1.0 / math.sqrt(GRID)))
    low = response.astype(jnp.bfloat16)
    for start in range(0, GRID, STEP):
        at = slice(start, start + STEP)
        orbitals = lax.dot_general(
            low, far_ref[at, :], (((1,), (1,)), ((), ())), preferred_element_type=jnp.float32
        )
        term = jnp.sum(own_ref[:, at].astype(jnp.float32) * orbitals, axis=0, keepdims=True)
        term = term * (1.0 / math.sqrt(BANDS))
        for block in range(STEP // LANES):
            row = start // LANES + block
            terms_ref[row : row + 1, :] = term[:, block * LANES : (block + 1) * LANES]
    return response


def to_far_order(value_ref, order_ref, column_ref, parts_ref):
    parts = in_parts(value_ref[...])
    rows = lax.broadcasted_iota(jnp.int32, (ROWS, LANES), 0)
    for block in range(ROWS):
        mine = (order_ref[block : block + 1, :] // LANES) == rows
        at = slice(block * LANES, (block + 1) * LANES)
        for index, part in enumerate(parts):
            wide = part[block : block + 1, :].astype(jnp.float32)
            parts_ref[index * ROWS : (index + 1) * ROWS, at] = jnp.where(mine, wide, 0.0).astype(jnp.bfloat16)
    sums = lax.dot_general(
        parts_ref[...], column_ref[...], (((1,), (1,)), ((), ())), preferred_element_type=jnp.float32
    )
    return sums[:ROWS] + sums[ROWS : 2 * ROWS] + sums[2 * ROWS :]


def from_far_order(value, order_ref, column_ref, out_ref, first_row):
    stacked = jnp.concatenate([part.astype(jnp.float32) for part in in_parts(value)]).astype(jnp.bfloat16)
    rows = lax.broadcasted_iota(jnp.int32, (ROWS, LANES), 0)
    for start in range(0, GRID, STEP):
        at = slice(start, start + STEP)
        spread = jnp.dot(stacked, column_ref[:, at], preferred_element_type=jnp.float32)
        spread = spread[:ROWS] + spread[ROWS : 2 * ROWS] + spread[2 * ROWS :]
        for block in range(STEP // LANES):
            row = start // LANES + block
            mine = (order_ref[row : row + 1, :] // LANES) == rows
            picked = jnp.where(mine, spread[:, block * LANES : (block + 1) * LANES], 0.0)
            out_ref[first_row + row : first_row + row + 1, :] = jnp.sum(picked, axis=0, keepdims=True)


UNROLL = 32


def prepare_kernel(order_smem, own_ref, order_ref, external_ref,
                   turned_ref, moved_ref, weighted_ref, column_ref, wide, scattered, parts, potential):
    wide[...] = own_ref[...].astype(jnp.float32)

    def move(step, carry):
        base = step * UNROLL
        for offset in range(UNROLL):
            row = base + offset
            scattered[pl.ds(order_smem[row], 1), :] = wide[pl.ds(row, 1), :]
        return carry

    lax.fori_loop(0, GRID // UNROLL, move, 0)
    columns = lax.broadcasted_iota(jnp.int32, (LANES, LANES), 0)

    def turn(block, carry):
        at = lane_block(block)
        turned_ref[:, at] = wide[at, :].T.astype(jnp.bfloat16)
        moved_ref[:, at] = scattered[at, :].T.astype(jnp.bfloat16)
        mine = (order_ref[pl.ds(block, 1), :] % LANES) == columns
        column_ref[:, at] = jnp.where(mine, 1.0, 0.0).astype(jnp.bfloat16)
        return carry

    lax.fori_loop(0, ROWS, turn, 0)
    potential[...] = to_far_order(external_ref, order_ref, column_ref, parts)
    weigh(potential, moved_ref, weighted_ref)


def second_kernel(order_smem, sent_ref, turned_ref, external_ref, energy_ref, far_energy_ref,
                  far_ref, terms_ref, wide, gathered, weighted):
    wide[...] = sent_ref[...].astype(jnp.float32)

    def move(step, carry):
        base = step * UNROLL
        for offset in range(UNROLL):
            row = base + offset
            gathered[pl.ds(row, 1), :] = wide[pl.ds(order_smem[row], 1), :]
        return carry

    lax.fori_loop(0, GRID // UNROLL, move, 0)
    far_ref[...] = gathered[...].astype(jnp.bfloat16)
    weigh(external_ref, turned_ref, weighted)
    respond(weighted, far_ref, turned_ref, weights(energy_ref[...], far_energy_ref[...]), terms_ref)


def first_kernel(flag_smem, *refs):
    piece_refs = refs[:4]
    (beside_ref, moved_ref, weighted_ref, order_ref, column_ref, energy_ref, far_energy_ref, other_ref,
     far_ref, terms_ref, own_terms) = refs[4:]

    @pl.when(flag_smem[0] == 1)
    def _():
        start = 0
        for piece in piece_refs:
            far_ref[start : start + piece.shape[0], :] = piece[...]
            start += piece.shape[0]

    @pl.when(flag_smem[0] == 0)
    def _():
        far_ref[...] = beside_ref[...]

    respond(weighted_ref, far_ref, moved_ref, weights(energy_ref[...], far_energy_ref[...]), own_terms)
    from_far_order(own_terms[...], order_ref, column_ref, terms_ref, 0)
    terms_ref[ROWS:, :] = other_ref[...]


def exact_dot(left, right):
    return jnp.dot(left, right, precision=lax.Precision.HIGHEST, preferred_element_type=jnp.float32)


def last_kernel(density_ref, external_ref, even_ref, odd_ref, into_ref, back_ref, screen_ref, even_t_ref, odd_t_ref,
                first_ref, second_ref, moved_ref, turned_ref, order_ref, column_ref,
                energy_ref, first_energy_ref, second_energy_ref,
                response_ref, terms_ref, parts, potential, moved_potential, weighted, own_terms):
    scale = 1.0 / math.sqrt(math.prod(AXIS_SIZES))
    low_half = lax.broadcasted_iota(jnp.int32, (ROWS, LANES), 1) < GY
    along_y = exact_dot(density_ref[...] * scale, into_ref[...])
    for q_index in range(NQ):
        at = slice(q_index * ROWS, (q_index + 1) * ROWS)
        spectrum = exact_dot(even_ref[...], along_y[at, :LANES]) + exact_dot(odd_ref[...], along_y[at, LANES:])
        back = exact_dot(spectrum * screen_ref[...], back_ref[...])
        field = jnp.where(low_half, exact_dot(even_t_ref[...], back), exact_dot(odd_t_ref[...], back))
        potential[at, :] = external_ref[...] + field
    moved_potential[...] = to_far_order(potential.at[0:ROWS], order_ref, column_ref, parts)
    weigh(moved_potential, moved_ref, weighted)
    weight = weights(energy_ref[...], first_energy_ref[...])
    response_ref[0] = respond(weighted, first_ref, moved_ref, weight, own_terms).T
    from_far_order(own_terms[...], order_ref, column_ref, terms_ref, 0)
    weigh(potential.at[ROWS : 2 * ROWS], turned_ref, weighted)
    weight = weights(energy_ref[...], second_energy_ref[...])
    response_ref[1] = respond(weighted, second_ref, turned_ref, weight, own_terms).T
    terms_ref[ROWS:, :] = own_terms[...]


def coulomb_tables():
    table = hartley_table(GX)
    other = hartley_table(GY)
    none = np.zeros((GY, 2 * GY))
    twice = np.concatenate([other, other], axis=1)
    into = np.concatenate([np.concatenate([twice, none]), np.concatenate([none, twice])], axis=1)
    back = np.concatenate([twice, none])
    screen = screening(GX, GY)
    screen = np.concatenate([screen, screen], axis=1)
    even, odd = table[:, 0::2], table[:, 1::2]
    return [part.astype(np.float32) for part in (even, odd, into, back, screen, even.T, odd.T)]


VMEM = pl.BlockSpec(memory_space=pltpu.VMEM)
SMEM = pl.BlockSpec(memory_space=pltpu.SMEM)


def local_call(kernel, smem, arrays, outs, scratch, microseconds):
    return pl.pallas_call(
        kernel,
        out_shape=[jax.ShapeDtypeStruct(shape, kind) for shape, kind in outs],
        in_specs=[SMEM] * smem + [VMEM] * (len(arrays) - smem),
        out_specs=[VMEM] * len(outs),
        scratch_shapes=[pltpu.VMEM(shape, kind) for shape, kind in scratch],
        cost_estimate=pl.CostEstimate(flops=0, bytes_accessed=microseconds * 3000000, transcendentals=0),
        compiler_params=pltpu.CompilerParams(vmem_limit_bytes=LIMIT),
    )(*arrays)


F32 = jnp.float32
BF16 = jnp.bfloat16
TALL = (GRID, BANDS)
TURNED = (BANDS, GRID)
BLOCKS = (ROWS, LANES)


def prepare(order, own, order_blocks, external):
    return local_call(
        prepare_kernel, 1, (order, own, order_blocks, external),
        [(TURNED, BF16)] * 3 + [((LANES, GRID), BF16)],
        [(TALL, F32), (TALL, F32), ((3 * ROWS, GRID), BF16), (BLOCKS, F32)], 12,
    )


def second_round_one(order, sent, turned, external, energy, far_energy):
    return local_call(
        second_kernel, 1, (order, sent, turned, external, energy, far_energy),
        [(TALL, BF16), (BLOCKS, F32)], [(TALL, F32), (TALL, F32), (TURNED, BF16)], 12,
    )


def first_round_one(flag, pieces, beside, moved, weighted, order_blocks, column, energy, far_energy, other):
    arrays = (flag, *pieces, beside, moved, weighted, order_blocks, column, energy, far_energy, other)
    return local_call(first_kernel, 1, arrays, [(TALL, BF16), ((2 * ROWS, LANES), F32)], [(BLOCKS, F32)], 3)


def round_two(density, external, first, second, moved, turned, order_blocks, column, energy, first_energy, second_energy):
    arrays = (density, external, *[jnp.asarray(part) for part in coulomb_tables()], first, second, moved, turned,
              order_blocks, column, energy, first_energy, second_energy)
    return local_call(
        last_kernel, 0, arrays,
        [((NQ, BANDS, BANDS), F32), ((2 * ROWS, LANES), F32)],
        [((3 * ROWS, GRID), BF16), ((2 * ROWS, LANES), F32), (BLOCKS, F32), (TURNED, BF16), (BLOCKS, F32)], 5,
    )


def exchange(value, axes):
    return lax.all_to_all(value, axes, 0, 0, tiled=True)


def summed_everywhere(value):
    plane = lax.axis_size(PLANE)
    column = lax.axis_size(COLUMN)
    chunks = value.reshape(plane, -1, LANES)
    part = jnp.sum(exchange(chunks, PLANE), axis=0)
    copies = jnp.broadcast_to(part[None], (column,) + part.shape)
    part = jnp.sum(exchange(copies, COLUMN), axis=0)
    copies = jnp.broadcast_to(part[None], (plane,) + part.shape)
    return exchange(copies, PLANE).reshape(value.shape)


def next_along(value, axis):
    count = lax.axis_size(axis)
    return lax.ppermute(value, axis, [(source, (source - 1) % count) for source in range(count)])


def iterate(states, energies, external, reorder):
    orbital = states[0]
    external = external.reshape(BLOCKS)
    order_blocks = reorder[0, 0].reshape(BLOCKS)
    column_index = lax.axis_index("x")

    cuts = (0, 1456, 2160, 2864, GRID)
    parts = [orbital[cuts[c] : cuts[c + 1]] for c in range(4)]
    count = lax.axis_size("zh")
    hops = [(4 * source, 4 * ((source - 1) % count)) for source in range(count)]
    hop0 = lax.ppermute(parts[0], KX, hops)
    spread = [lax.ppermute(parts[c], "x", [(0, c)]) for c in range(1, 4)]
    far_second = next_along(orbital, KY)
    beside = lax.ppermute(orbital, "x", [(1, 0), (2, 1), (3, 2)])
    inner = jnp.where(column_index == 1, spread[0], spread[1])
    outer, inner, own = lax.optimization_barrier((spread[2], inner, orbital))
    hop3 = lax.ppermute(outer, KX, [(s + 3, t + 3) for s, t in hops])
    hop12 = lax.ppermute(inner, KX, [(s + x, t + x) for s, t in hops for x in (1, 2)])
    second_energy = next_along(energies, KY)
    first_energy = next_along(energies, KX)

    turned, moved, weighted, column = prepare(reorder[0, 0], own, order_blocks, external)
    second_states, second_terms = second_round_one(
        reorder[1, 0], far_second, turned, external, energies, second_energy
    )

    second_terms, hop0, hop12, hop3 = lax.optimization_barrier((second_terms, hop0, hop12, hop3))
    pieces = [lax.ppermute(hop0, "x", [(0, 3)])]
    pieces += [lax.ppermute(hop12, "x", [(x, 3)]) for x in (1, 2)]
    flag = (column_index == 3).astype(jnp.int32).reshape(1)
    first_states, terms = first_round_one(
        flag, pieces + [hop3], beside, moved, weighted, order_blocks, column, energies, first_energy, second_terms
    )
    response, terms = round_two(
        summed_everywhere(terms), external, first_states, second_states, moved, turned, order_blocks, column,
        energies, first_energy, second_energy,
    )
    density = summed_everywhere(terms) * (1.0 / math.sqrt(lax.axis_size(AXES)))
    return (response.reshape(1, NQ, 1, BANDS, BANDS), density.reshape(NQ, 1, GRID))


def solution(mesh):
    fine = Mesh(mesh.devices.reshape(AXIS_SIZES), AXES)
    return jax.shard_map(
        iterate,
        mesh=fine,
        in_specs=(
            P(AXES, None, None),
            P(AXES, None),
            P(),
            P(None, AXES, None),
        ),
        out_specs=(P(AXES, None, None, None, None), P()),
        check_vma=False,
    )
```

```python
import math

import jax
import jax.numpy as jnp
import numpy as np
from jax import lax
from jax.experimental import pallas as pl
from jax.experimental.pallas import tpu as pltpu
from jax.sharding import Mesh, PartitionSpec as P


AXES = ("zh", "x", "y", "zl", "core")
AXIS_SIZES = (4, 4, 4, 4, 2)
KX = ("zh", "x")
KY = ("y", "zl", "core")
PLANE = ("x", "y", "core")
COLUMN = ("zh", "zl")

GX = 64
GY = 64
NQ = 2
GRID = GX * GY
BANDS = 128
LANES = 128
ROWS = GRID // LANES
STEP = 512

SMEAR = 0.5
FERMI = 0.0
SCREEN = 4.0


def hartley_table(length):
    positions = np.arange(length)
    angles = positions[:, None] * positions[None, :] % length * (2.0 * math.pi / length)
    return (np.cos(angles) + np.sin(angles)) / math.sqrt(length)


def screening(len_x, len_y):
    freq_x = np.arange(len_x)
    freq_x = np.minimum(freq_x, len_x - freq_x)
    freq_y = np.arange(len_y)
    freq_y = np.minimum(freq_y, len_y - freq_y)
    return 1.0 / (1.0 + (freq_x[:, None] ** 2 + freq_y[None, :] ** 2) / SCREEN)


def lane_block(index):
    return pl.ds(pl.multiple_of(index * LANES, LANES), LANES)


def in_parts(value):
    high = value.astype(jnp.bfloat16)
    rest = value - high.astype(jnp.float32)
    middle = rest.astype(jnp.bfloat16)
    low = (rest - middle.astype(jnp.float32)).astype(jnp.bfloat16)
    return (high, middle, low)


def occupation(energy):
    return 1.0 / (1.0 + jnp.exp((energy - FERMI) / SMEAR))


def across(row):
    return jnp.broadcast_to(row, (BANDS, BANDS)).T


def weights(energy, far_energy):
    energy = energy.astype(jnp.float32)
    far_energy = far_energy.astype(jnp.float32)
    gap = far_energy - across(energy)
    filled = across(occupation(energy)) - occupation(far_energy)
    return filled * gap / (gap * gap + SMEAR * SMEAR)


def weigh(potential_ref, own_ref, weighted_ref):
    for block in range(ROWS):
        at = slice(block * LANES, (block + 1) * LANES)
        product = potential_ref[block : block + 1, :] * own_ref[:, at].astype(jnp.float32)
        weighted_ref[:, at] = product.astype(jnp.bfloat16)


def respond(weighted_ref, far_ref, own_ref, weight, terms_ref):
    bands = jnp.zeros((BANDS, BANDS), jnp.float32)
    for start in range(0, GRID, STEP):
        at = slice(start, start + STEP)
        bands += jnp.dot(weighted_ref[:, at], far_ref[at, :], preferred_element_type=jnp.float32)
    response = weight * (bands * (1.0 / math.sqrt(GRID)))
    low = response.astype(jnp.bfloat16)
    for start in range(0, GRID, STEP):
        at = slice(start, start + STEP)
        orbitals = lax.dot_general(
            low, far_ref[at, :], (((1,), (1,)), ((), ())), preferred_element_type=jnp.float32
        )
        term = jnp.sum(own_ref[:, at].astype(jnp.float32) * orbitals, axis=0, keepdims=True)
        term = term * (1.0 / math.sqrt(BANDS))
        for block in range(STEP // LANES):
            row = start // LANES + block
            terms_ref[row : row + 1, :] = term[:, block * LANES : (block + 1) * LANES]
    return response


def to_far_order(value_ref, order_ref, column_ref, parts_ref):
    parts = in_parts(value_ref[...])
    rows = lax.broadcasted_iota(jnp.int32, (ROWS, LANES), 0)
    for block in range(ROWS):
        mine = (order_ref[block : block + 1, :] // LANES) == rows
        at = slice(block * LANES, (block + 1) * LANES)
        for index, part in enumerate(parts):
            wide = part[block : block + 1, :].astype(jnp.float32)
            parts_ref[index * ROWS : (index + 1) * ROWS, at] = jnp.where(mine, wide, 0.0).astype(jnp.bfloat16)
    sums = lax.dot_general(
        parts_ref[...], column_ref[...], (((1,), (1,)), ((), ())), preferred_element_type=jnp.float32
    )
    return sums[:ROWS] + sums[ROWS : 2 * ROWS] + sums[2 * ROWS :]


def from_far_order(value, order_ref, column_ref, out_ref, first_row):
    stacked = jnp.concatenate([part.astype(jnp.float32) for part in in_parts(value)]).astype(jnp.bfloat16)
    rows = lax.broadcasted_iota(jnp.int32, (ROWS, LANES), 0)
    for start in range(0, GRID, STEP):
        at = slice(start, start + STEP)
        spread = jnp.dot(stacked, column_ref[:, at], preferred_element_type=jnp.float32)
        spread = spread[:ROWS] + spread[ROWS : 2 * ROWS] + spread[2 * ROWS :]
        for block in range(STEP // LANES):
            row = start // LANES + block
            mine = (order_ref[row : row + 1, :] // LANES) == rows
            picked = jnp.where(mine, spread[:, block * LANES : (block + 1) * LANES], 0.0)
            out_ref[first_row + row : first_row + row + 1, :] = jnp.sum(picked, axis=0, keepdims=True)


UNROLL = 32


def started(sems, *pairs, first=0):
    copies = []
    for index, (source, target) in enumerate(pairs):
        copies.append(pltpu.make_async_copy(source, target, sems.at[first + index]))
        copies[-1].start()
    return copies


def finished(copies):
    for copy in copies:
        copy.wait()


def prepare_kernel(order_smem, own_ref, order_ref, external_ref,
                   turned_out, moved_out, weighted_out, column_out,
                   turned_ref, moved_ref, weighted_ref, column_ref, wide, scattered, parts, potential, sems):
    wide[...] = own_ref[...].astype(jnp.float32)

    def move(step, carry):
        base = step * UNROLL
        for offset in range(UNROLL):
            row = base + offset
            scattered[pl.ds(order_smem[row], 1), :] = wide[pl.ds(row, 1), :]
        return carry

    lax.fori_loop(0, GRID // UNROLL, move, 0)
    columns = lax.broadcasted_iota(jnp.int32, (LANES, LANES), 0)

    def turn(block, carry):
        at = lane_block(block)
        turned_ref[:, at] = wide[at, :].T.astype(jnp.bfloat16)
        moved_ref[:, at] = scattered[at, :].T.astype(jnp.bfloat16)
        mine = (order_ref[pl.ds(block, 1), :] % LANES) == columns
        column_ref[:, at] = jnp.where(mine, 1.0, 0.0).astype(jnp.bfloat16)
        return carry

    lax.fori_loop(0, ROWS, turn, 0)
    copies = started(sems, (turned_ref, turned_out), (moved_ref, moved_out), (column_ref, column_out))
    potential[...] = to_far_order(external_ref, order_ref, column_ref, parts)
    weigh(potential, moved_ref, weighted_ref)
    copies += started(sems, (weighted_ref, weighted_out), first=3)
    finished(copies)


def second_kernel(order_smem, sent_ref, turned_in, external_ref, energy_ref, far_energy_ref,
                  far_out, terms_ref, wide, gathered, weighted, turned_ref, far_ref, sems):
    loads = started(sems, (turned_in, turned_ref))
    wide[...] = sent_ref[...].astype(jnp.float32)

    def move(step, carry):
        base = step * UNROLL
        for offset in range(UNROLL):
            row = base + offset
            gathered[pl.ds(row, 1), :] = wide[pl.ds(order_smem[row], 1), :]
        return carry

    lax.fori_loop(0, GRID // UNROLL, move, 0)
    far_ref[...] = gathered[...].astype(jnp.bfloat16)
    stores = started(sems, (far_ref, far_out), first=1)
    finished(loads)
    weigh(external_ref, turned_ref, weighted)
    respond(weighted, far_ref, turned_ref, weights(energy_ref[...], far_energy_ref[...]), terms_ref)
    finished(stores)


def first_kernel(flag_smem, *refs):
    piece_refs = refs[:4]
    (beside_ref, moved_in, weighted_in, order_ref, column_in, energy_ref, far_energy_ref, other_ref,
     far_out, terms_ref, own_terms, far_ref, moved_ref, weighted_ref, column_ref, sems) = refs[4:]
    loads = started(sems, (weighted_in, weighted_ref), (moved_in, moved_ref), (column_in, column_ref))

    @pl.when(flag_smem[0] == 1)
    def _():
        start, pairs = 0, []
        for piece in piece_refs:
            pairs.append((piece, far_ref.at[pl.ds(start, piece.shape[0])]))
            start += piece.shape[0]
        finished(started(sems, *pairs, first=4))

    @pl.when(flag_smem[0] == 0)
    def _():
        finished(started(sems, (beside_ref, far_ref), first=8))

    stores = started(sems, (far_ref, far_out), first=3)
    weight = weights(energy_ref[...], far_energy_ref[...])
    finished(loads)
    respond(weighted_ref, far_ref, moved_ref, weight, own_terms)
    from_far_order(own_terms[...], order_ref, column_ref, terms_ref, 0)
    terms_ref[ROWS:, :] = other_ref[...]
    finished(stores)


def exact_dot(left, right):
    return jnp.dot(left, right, precision=lax.Precision.HIGHEST, preferred_element_type=jnp.float32)


def last_kernel(density_ref, external_ref, even_ref, odd_ref, into_ref, back_ref, screen_ref, even_t_ref, odd_t_ref,
                first_in, second_in, moved_in, turned_in, order_ref, column_in,
                energy_ref, first_energy_ref, second_energy_ref,
                response_ref, terms_ref, parts, potential, moved_potential, weighted, own_terms,
                first_ref, second_ref, moved_ref, turned_ref, column_ref, sems):
    loads = started(sems, (column_in, column_ref), (moved_in, moved_ref), (first_in, first_ref))
    later = started(sems, (turned_in, turned_ref), (second_in, second_ref), first=3)
    scale = 1.0 / math.sqrt(math.prod(AXIS_SIZES))
    low_half = lax.broadcasted_iota(jnp.int32, (ROWS, LANES), 1) < GY
    along_y = exact_dot(density_ref[...] * scale, into_ref[...])
    for q_index in range(NQ):
        at = slice(q_index * ROWS, (q_index + 1) * ROWS)
        spectrum = exact_dot(even_ref[...], along_y[at, :LANES]) + exact_dot(odd_ref[...], along_y[at, LANES:])
        back = exact_dot(spectrum * screen_ref[...], back_ref[...])
        field = jnp.where(low_half, exact_dot(even_t_ref[...], back), exact_dot(odd_t_ref[...], back))
        potential[at, :] = external_ref[...] + field
    finished(loads)
    moved_potential[...] = to_far_order(potential.at[0:ROWS], order_ref, column_ref, parts)
    weigh(moved_potential, moved_ref, weighted)
    weight = weights(energy_ref[...], first_energy_ref[...])
    response_ref[0] = respond(weighted, first_ref, moved_ref, weight, own_terms).T
    from_far_order(own_terms[...], order_ref, column_ref, terms_ref, 0)
    finished(later)
    weigh(potential.at[ROWS : 2 * ROWS], turned_ref, weighted)
    weight = weights(energy_ref[...], second_energy_ref[...])
    response_ref[1] = respond(weighted, second_ref, turned_ref, weight, own_terms).T
    terms_ref[ROWS:, :] = own_terms[...]


def coulomb_tables():
    table = hartley_table(GX)
    other = hartley_table(GY)
    none = np.zeros((GY, 2 * GY))
    twice = np.concatenate([other, other], axis=1)
    into = np.concatenate([np.concatenate([twice, none]), np.concatenate([none, twice])], axis=1)
    back = np.concatenate([twice, none])
    screen = screening(GX, GY)
    screen = np.concatenate([screen, screen], axis=1)
    even, odd = table[:, 0::2], table[:, 1::2]
    return [part.astype(np.float32) for part in (even, odd, into, back, screen, even.T, odd.T)]


VMEM = pl.BlockSpec(memory_space=pltpu.VMEM)
SMEM = pl.BlockSpec(memory_space=pltpu.SMEM)
HBM = pl.BlockSpec(memory_space=pltpu.HBM)


def local_call(kernel, arrays, in_specs, outs, scratch, copies, microseconds):
    return pl.pallas_call(
        kernel,
        out_shape=[jax.ShapeDtypeStruct(shape, kind) for shape, kind, spec in outs],
        in_specs=in_specs,
        out_specs=[spec for shape, kind, spec in outs],
        scratch_shapes=[pltpu.VMEM(shape, kind) for shape, kind in scratch] + [pltpu.SemaphoreType.DMA((copies,))],
        cost_estimate=pl.CostEstimate(flops=0, bytes_accessed=microseconds * 3000000, transcendentals=0),
    )(*arrays)


F32 = jnp.float32
BF16 = jnp.bfloat16
TALL = (GRID, BANDS)
TURNED = (BANDS, GRID)
BLOCKS = (ROWS, LANES)


def prepare(order, own, order_blocks, external):
    return local_call(
        prepare_kernel, (order, own, order_blocks, external), [SMEM, VMEM, VMEM, VMEM],
        [(TURNED, BF16, HBM)] * 4,
        [(TURNED, BF16)] * 4 + [(TALL, F32), (TALL, F32), ((3 * ROWS, GRID), BF16), (BLOCKS, F32)], 4, 10,
    )


def second_round_one(order, sent, turned, external, energy, far_energy):
    return local_call(
        second_kernel, (order, sent, turned, external, energy, far_energy),
        [SMEM, VMEM, HBM, VMEM, VMEM, VMEM],
        [(TALL, BF16, HBM), (BLOCKS, F32, VMEM)],
        [(TALL, F32), (TALL, F32), (TURNED, BF16), (TURNED, BF16), (TALL, BF16)], 2, 7,
    )


def first_round_one(flag, pieces, beside, moved, weighted, order_blocks, column, energy, far_energy, other):
    arrays = (flag, *pieces, beside, moved, weighted, order_blocks, column, energy, far_energy, other)
    return local_call(
        first_kernel, arrays, [SMEM] + [HBM] * 5 + [HBM, HBM, VMEM, HBM, VMEM, VMEM, VMEM],
        [(TALL, BF16, HBM), ((2 * ROWS, LANES), F32, VMEM)],
        [(BLOCKS, F32), (TALL, BF16)] + [(TURNED, BF16)] * 3, 9, 3,
    )


def round_two(density, external, first, second, moved, turned, order_blocks, column, energy, first_energy, second_energy):
    arrays = (density, external, *[jnp.asarray(part) for part in coulomb_tables()], first, second, moved, turned,
              order_blocks, column, energy, first_energy, second_energy)
    return local_call(
        last_kernel, arrays, [VMEM] * 9 + [HBM] * 4 + [VMEM, HBM, VMEM, VMEM, VMEM],
        [((NQ, BANDS, BANDS), F32, VMEM), ((2 * ROWS, LANES), F32, VMEM)],
        [((3 * ROWS, GRID), BF16), ((2 * ROWS, LANES), F32), (BLOCKS, F32), (TURNED, BF16), (BLOCKS, F32)]
        + [(TALL, BF16)] * 2 + [(TURNED, BF16)] * 3, 5, 5,
    )


def exchange(value, axes):
    return lax.all_to_all(value, axes, 0, 0, tiled=True)


def summed_everywhere(value):
    plane = lax.axis_size(PLANE)
    column = lax.axis_size(COLUMN)
    chunks = value.reshape(plane, -1, LANES)
    part = jnp.sum(exchange(chunks, PLANE), axis=0)
    copies = jnp.broadcast_to(part[None], (column,) + part.shape)
    part = jnp.sum(exchange(copies, COLUMN), axis=0)
    copies = jnp.broadcast_to(part[None], (plane,) + part.shape)
    return exchange(copies, PLANE).reshape(value.shape)


def next_along(value, axis):
    count = lax.axis_size(axis)
    return lax.ppermute(value, axis, [(source, (source - 1) % count) for source in range(count)])


def iterate(states, energies, external, reorder):
    orbital = states[0]
    external = external.reshape(BLOCKS)
    order_blocks = reorder[0, 0].reshape(BLOCKS)
    column_index = lax.axis_index("x")

    cuts = (0, 1360, 2064, 2768, GRID)
    parts = [orbital[cuts[c] : cuts[c + 1]] for c in range(4)]
    count = lax.axis_size("zh")
    hops = [(4 * source, 4 * ((source - 1) % count)) for source in range(count)]
    hop0 = lax.ppermute(parts[0], KX, hops)
    spread = [lax.ppermute(parts[c], "x", [(0, c)]) for c in range(1, 4)]
    far_second = next_along(orbital, KY)
    beside = lax.ppermute(orbital, "x", [(1, 0), (2, 1), (3, 2)])
    inner = jnp.where(column_index == 1, spread[0], spread[1])
    outer, inner, own = lax.optimization_barrier((spread[2], inner, orbital))
    hop3 = lax.ppermute(outer, KX, [(s + 3, t + 3) for s, t in hops])
    hop12 = lax.ppermute(inner, KX, [(s + x, t + x) for s, t in hops for x in (1, 2)])
    second_energy = next_along(energies, KY)
    first_energy = next_along(energies, KX)

    turned, moved, weighted, column = prepare(reorder[0, 0], own, order_blocks, external)
    column, hop0, hop12, hop3 = lax.optimization_barrier((column, hop0, hop12, hop3))
    pieces = [lax.ppermute(hop0, "x", [(0, 3)])]
    pieces += [lax.ppermute(hop12, "x", [(x, 3)]) for x in (1, 2)]
    second_states, second_terms = second_round_one(reorder[1, 0], far_second, turned, external, energies, second_energy)
    flag = (column_index == 3).astype(jnp.int32).reshape(1)
    first_states, terms = first_round_one(
        flag, pieces + [hop3], beside, moved, weighted, order_blocks, column, energies, first_energy, second_terms
    )
    response, terms = round_two(
        summed_everywhere(terms), external, first_states, second_states, moved, turned, order_blocks, column,
        energies, first_energy, second_energy,
    )
    density = summed_everywhere(terms) * (1.0 / math.sqrt(lax.axis_size(AXES)))
    return (response.reshape(1, NQ, 1, BANDS, BANDS), density.reshape(NQ, 1, GRID))


def solution(mesh):
    fine = Mesh(mesh.devices.reshape(AXIS_SIZES), AXES)
    return jax.shard_map(
        iterate,
        mesh=fine,
        in_specs=(
            P(AXES, None, None),
            P(AXES, None),
            P(),
            P(None, AXES, None),
        ),
        out_specs=(P(AXES, None, None, None, None), P()),
        check_vma=False,
    )
```

```python
import math

import jax
import jax.numpy as jnp
import numpy as np
from jax import lax
from jax.experimental import pallas as pl
from jax.experimental.pallas import tpu as pltpu
from jax.sharding import Mesh, PartitionSpec as P


AXES = ("zh", "x", "y", "zl", "core")
AXIS_SIZES = (4, 4, 4, 4, 2)
KX = ("zh", "x")
KY = ("y", "zl", "core")
PLANE = ("x", "y", "core")
COLUMN = ("zh", "zl")

GX = 64
GY = 64
NQ = 2
GRID = GX * GY
BANDS = 128
LANES = 128
ROWS = GRID // LANES
STEP = 512
LIMIT = 24 * 1024 * 1024

SMEAR = 0.5
FERMI = 0.0
SCREEN = 4.0


def hartley_table(length):
    positions = np.arange(length)
    angles = positions[:, None] * positions[None, :] % length * (2.0 * math.pi / length)
    return (np.cos(angles) + np.sin(angles)) / math.sqrt(length)


def screening(len_x, len_y):
    freq_x = np.arange(len_x)
    freq_x = np.minimum(freq_x, len_x - freq_x)
    freq_y = np.arange(len_y)
    freq_y = np.minimum(freq_y, len_y - freq_y)
    return 1.0 / (1.0 + (freq_x[:, None] ** 2 + freq_y[None, :] ** 2) / SCREEN)


def lane_block(index):
    return pl.ds(pl.multiple_of(index * LANES, LANES), LANES)


def in_parts(value):
    high = value.astype(jnp.bfloat16)
    rest = value - high.astype(jnp.float32)
    middle = rest.astype(jnp.bfloat16)
    low = (rest - middle.astype(jnp.float32)).astype(jnp.bfloat16)
    return (high, middle, low)


def occupation(energy):
    return 1.0 / (1.0 + jnp.exp((energy - FERMI) / SMEAR))


def across(row):
    return jnp.broadcast_to(row, (BANDS, BANDS)).T


def weights(energy, far_energy):
    energy = energy.astype(jnp.float32)
    far_energy = far_energy.astype(jnp.float32)
    gap = far_energy - across(energy)
    filled = across(occupation(energy)) - occupation(far_energy)
    return filled * gap / (gap * gap + SMEAR * SMEAR)


def weigh(potential_ref, own_ref, weighted_ref):
    for block in range(ROWS):
        at = slice(block * LANES, (block + 1) * LANES)
        product = potential_ref[block : block + 1, :] * own_ref[:, at].astype(jnp.float32)
        weighted_ref[:, at] = product.astype(jnp.bfloat16)


def respond(weighted_ref, far_ref, own_ref, weight, terms_ref):
    points = math.prod(AXIS_SIZES)
    bands = jnp.zeros((BANDS, BANDS), jnp.float32)
    for start in range(0, GRID, STEP):
        at = slice(start, start + STEP)
        bands += jnp.dot(weighted_ref[:, at], far_ref[at, :], preferred_element_type=jnp.float32)
    response = weight * (bands * (1.0 / math.sqrt(GRID)))
    low = response.astype(jnp.bfloat16)
    for start in range(0, GRID, STEP):
        at = slice(start, start + STEP)
        orbitals = lax.dot_general(
            low, far_ref[at, :], (((1,), (1,)), ((), ())), preferred_element_type=jnp.float32
        )
        term = jnp.sum(own_ref[:, at].astype(jnp.float32) * orbitals, axis=0, keepdims=True)
        term = term * (1.0 / math.sqrt(BANDS * points))
        for block in range(STEP // LANES):
            row = start // LANES + block
            terms_ref[row : row + 1, :] = term[:, block * LANES : (block + 1) * LANES]
    return response


def mark_columns(order_ref, column_ref):
    columns = lax.broadcasted_iota(jnp.int32, (LANES, LANES), 0)
    for block in range(ROWS):
        mine = (order_ref[block : block + 1, :] % LANES) == columns
        column_ref[:, block * LANES : (block + 1) * LANES] = jnp.where(mine, 1.0, 0.0).astype(jnp.bfloat16)


def to_far_order(value_ref, order_ref, column_ref, parts_ref):
    parts = in_parts(value_ref[...])
    rows = lax.broadcasted_iota(jnp.int32, (ROWS, LANES), 0)
    for block in range(ROWS):
        mine = (order_ref[block : block + 1, :] // LANES) == rows
        at = slice(block * LANES, (block + 1) * LANES)
        for index, part in enumerate(parts):
            wide = part[block : block + 1, :].astype(jnp.float32)
            parts_ref[index * ROWS : (index + 1) * ROWS, at] = jnp.where(mine, wide, 0.0).astype(jnp.bfloat16)
    sums = lax.dot_general(
        parts_ref[...], column_ref[...], (((1,), (1,)), ((), ())), preferred_element_type=jnp.float32
    )
    return sums[:ROWS] + sums[ROWS : 2 * ROWS] + sums[2 * ROWS :]


def from_far_order(value, order_ref, column_ref, out_ref, first_row):
    stacked = jnp.concatenate([part.astype(jnp.float32) for part in in_parts(value)]).astype(jnp.bfloat16)
    rows = lax.broadcasted_iota(jnp.int32, (ROWS, LANES), 0)
    for start in range(0, GRID, STEP):
        at = slice(start, start + STEP)
        spread = jnp.dot(stacked, column_ref[:, at], preferred_element_type=jnp.float32)
        spread = spread[:ROWS] + spread[ROWS : 2 * ROWS] + spread[2 * ROWS :]
        for block in range(STEP // LANES):
            row = start // LANES + block
            mine = (order_ref[row : row + 1, :] // LANES) == rows
            picked = jnp.where(mine, spread[:, block * LANES : (block + 1) * LANES], 0.0)
            out_ref[first_row + row : first_row + row + 1, :] = jnp.sum(picked, axis=0, keepdims=True)


UNROLL = 32


def started(sems, *pairs, first=0):
    copies = []
    for index, (source, target) in enumerate(pairs):
        copies.append(pltpu.make_async_copy(source, target, sems.at[first + index]))
        copies[-1].start()
    return copies


def finished(copies):
    for copy in copies:
        copy.wait()


def prepare_kernel(order_smem, own_ref, order_ref, external_ref,
                   turned_ref, moved_ref, potential_ref, turned_out, moved_out,
                   wide, scattered, parts, column, sems):
    wide[...] = own_ref[...].astype(jnp.float32)

    def move(step, carry):
        base = step * UNROLL
        for offset in range(UNROLL):
            row = base + offset
            scattered[pl.ds(order_smem[row], 1), :] = wide[pl.ds(row, 1), :]
        return carry

    lax.fori_loop(0, GRID // UNROLL, move, 0)

    def turn(block, carry):
        at = lane_block(block)
        turned_ref[:, at] = wide[at, :].T.astype(jnp.bfloat16)
        moved_ref[:, at] = scattered[at, :].T.astype(jnp.bfloat16)
        return carry

    lax.fori_loop(0, ROWS, turn, 0)
    copies = started(sems, (turned_ref, turned_out), (moved_ref, moved_out))
    mark_columns(order_ref, column)
    potential_ref[...] = to_far_order(external_ref, order_ref, column, parts)
    finished(copies)


def second_kernel(order_smem, sent_ref, turned_ref, external_ref, energy_ref, far_energy_ref,
                  far_out, terms_ref, wide, gathered, weighted, far_ref, sems):
    wide[...] = sent_ref[...].astype(jnp.float32)

    def move(step, carry):
        base = step * UNROLL
        for offset in range(UNROLL):
            row = base + offset
            gathered[pl.ds(row, 1), :] = wide[pl.ds(order_smem[row], 1), :]
        return carry

    lax.fori_loop(0, GRID // UNROLL, move, 0)
    far_ref[...] = gathered[...].astype(jnp.bfloat16)
    stores = started(sems, (far_ref, far_out))
    weigh(external_ref, turned_ref, weighted)
    respond(weighted, far_ref, turned_ref, weights(energy_ref[...], far_energy_ref[...]), terms_ref)
    finished(stores)


def first_kernel(flag_smem, *refs):
    piece_refs = refs[:4]
    (beside_ref, moved_ref, potential_ref, order_ref, energy_ref, far_energy_ref, other_ref,
     far_out, terms_ref, own_terms, far_ref, weighted_ref, column_ref, sems) = refs[4:]

    @pl.when(flag_smem[0] == 1)
    def _():
        last = piece_refs[3]
        start = GRID - last.shape[0]
        copies = started(sems, (last, far_ref.at[pl.ds(start, last.shape[0])]), first=1)
        start = 0
        for piece in piece_refs[:3]:
            far_ref[start : start + piece.shape[0], :] = piece[...]
            start += piece.shape[0]
        finished(copies)

    @pl.when(flag_smem[0] == 0)
    def _():
        far_ref[...] = beside_ref[...]

    stores = started(sems, (far_ref, far_out))
    weight = weights(energy_ref[...], far_energy_ref[...])
    weigh(potential_ref, moved_ref, weighted_ref)
    mark_columns(order_ref, column_ref)
    respond(weighted_ref, far_ref, moved_ref, weight, own_terms)
    from_far_order(own_terms[...], order_ref, column_ref, terms_ref, 0)
    terms_ref[ROWS:, :] = other_ref[...]
    finished(stores)


def exact_dot(left, right):
    return jnp.dot(left, right, precision=lax.Precision.HIGHEST, preferred_element_type=jnp.float32)


def last_kernel(density_ref, external_ref, even_ref, odd_ref, into_ref, back_ref, screen_ref, even_t_ref, odd_t_ref,
                first_in, second_in, moved_in, turned_in, order_ref,
                energy_ref, first_energy_ref, second_energy_ref,
                response_ref, terms_ref, parts, potential, moved_potential, weighted, own_terms,
                first_ref, second_ref, moved_ref, turned_ref, column_ref, sems):
    loads = started(sems, (moved_in, moved_ref), (first_in, first_ref))
    later = started(sems, (turned_in, turned_ref), (second_in, second_ref), first=2)
    mark_columns(order_ref, column_ref)
    low_half = lax.broadcasted_iota(jnp.int32, (ROWS, LANES), 1) < GY
    along_y = exact_dot(density_ref[...], into_ref[...])
    for q_index in range(NQ):
        at = slice(q_index * ROWS, (q_index + 1) * ROWS)
        spectrum = exact_dot(even_ref[...], along_y[at, :LANES]) + exact_dot(odd_ref[...], along_y[at, LANES:])
        back = exact_dot(spectrum * screen_ref[...], back_ref[...])
        field = jnp.where(low_half, exact_dot(even_t_ref[...], back), exact_dot(odd_t_ref[...], back))
        potential[at, :] = external_ref[...] + field
    moved_potential[...] = to_far_order(potential.at[0:ROWS], order_ref, column_ref, parts)
    finished(loads)
    weigh(moved_potential, moved_ref, weighted)
    weight = weights(energy_ref[...], first_energy_ref[...])
    response_ref[0] = respond(weighted, first_ref, moved_ref, weight, own_terms).T
    from_far_order(own_terms[...], order_ref, column_ref, terms_ref, 0)
    finished(later)
    weigh(potential.at[ROWS : 2 * ROWS], turned_ref, weighted)
    weight = weights(energy_ref[...], second_energy_ref[...])
    response_ref[1] = respond(weighted, second_ref, turned_ref, weight, own_terms).T
    terms_ref[ROWS:, :] = own_terms[...]


def coulomb_tables():
    table = hartley_table(GX)
    other = hartley_table(GY)
    none = np.zeros((GY, 2 * GY))
    twice = np.concatenate([other, other], axis=1)
    into = np.concatenate([np.concatenate([twice, none]), np.concatenate([none, twice])], axis=1)
    back = np.concatenate([twice, none])
    screen = screening(GX, GY)
    screen = np.concatenate([screen, screen], axis=1)
    even, odd = table[:, 0::2], table[:, 1::2]
    return [part.astype(np.float32) for part in (even, odd, into, back, screen, even.T, odd.T)]


VMEM = pl.BlockSpec(memory_space=pltpu.VMEM)
SMEM = pl.BlockSpec(memory_space=pltpu.SMEM)
HBM = pl.BlockSpec(memory_space=pltpu.HBM)
KEPT = pl.BlockSpec(memory_space=pltpu.VMEM)
PLACES = {id(HBM): pltpu.HBM, id(KEPT): pltpu.VMEM}


def local_call(kernel, arrays, in_specs, outs, scratch, copies, microseconds, limit=None):
    return pl.pallas_call(
        kernel,
        out_shape=[
            PLACES.get(id(spec), jax.ShapeDtypeStruct)(shape, kind) for shape, kind, spec in outs
        ],
        in_specs=in_specs,
        out_specs=[spec for shape, kind, spec in outs],
        scratch_shapes=[pltpu.VMEM(shape, kind) for shape, kind in scratch] + [pltpu.SemaphoreType.DMA((copies,))],
        cost_estimate=pl.CostEstimate(flops=0, bytes_accessed=microseconds * 3000000, transcendentals=0),
        compiler_params=pltpu.CompilerParams(vmem_limit_bytes=limit),
    )(*arrays)


F32 = jnp.float32
BF16 = jnp.bfloat16
TALL = (GRID, BANDS)
TURNED = (BANDS, GRID)
BLOCKS = (ROWS, LANES)


def prepare(order, own, order_blocks, external):
    return local_call(
        prepare_kernel, (order, own, order_blocks, external), [SMEM, VMEM, VMEM, VMEM],
        [(TURNED, BF16, KEPT)] * 2 + [(BLOCKS, F32, VMEM)] + [(TURNED, BF16, HBM)] * 2,
        [(TALL, F32), (TALL, F32), ((3 * ROWS, GRID), BF16), (TURNED, BF16)], 2, 10,
        LIMIT,
    )


def second_round_one(order, sent, turned, external, energy, far_energy):
    sent = pltpu.with_memory_space_constraint(sent, pltpu.VMEM)
    turned = pltpu.with_memory_space_constraint(turned, pltpu.VMEM)
    return local_call(
        second_kernel, (order, sent, turned, external, energy, far_energy),
        [SMEM, VMEM, VMEM, VMEM, VMEM, VMEM],
        [(TALL, BF16, HBM), (BLOCKS, F32, VMEM)],
        [(TALL, F32), (TALL, F32), (TURNED, BF16), (TALL, BF16)], 1, 7, LIMIT,
    )


def first_round_one(flag, pieces, beside, moved, potential, order_blocks, energy, far_energy, other):
    places = [pltpu.VMEM] * 3 + [pltpu.HBM]
    pieces = [pltpu.with_memory_space_constraint(piece, place) for piece, place in zip(pieces, places)]
    beside = pltpu.with_memory_space_constraint(beside, pltpu.VMEM)
    moved = pltpu.with_memory_space_constraint(moved, pltpu.VMEM)
    return local_call(
        first_kernel, (flag, *pieces, beside, moved, potential, order_blocks, energy, far_energy, other),
        [SMEM] + [VMEM] * 3 + [HBM] + [VMEM] * 7,
        [(TALL, BF16, HBM), ((2 * ROWS, LANES), F32, VMEM)],
        [(BLOCKS, F32), (TALL, BF16), (TURNED, BF16), (TURNED, BF16)], 2, 3, LIMIT,
    )


def round_two(density, external, first, second, moved, turned, order_blocks, energy, first_energy, second_energy):
    arrays = (density, external, *[jnp.asarray(part) for part in coulomb_tables()], first, second, moved, turned,
              order_blocks, energy, first_energy, second_energy)
    return local_call(
        last_kernel, arrays, [VMEM] * 9 + [HBM] * 4 + [VMEM] * 4,
        [((NQ, BANDS, BANDS), F32, VMEM), ((2 * ROWS, LANES), F32, VMEM)],
        [((3 * ROWS, GRID), BF16), ((2 * ROWS, LANES), F32), (BLOCKS, F32), (TURNED, BF16), (BLOCKS, F32)]
        + [(TALL, BF16)] * 2 + [(TURNED, BF16)] * 3, 4, 5,
    )


def exchange(value, axes):
    return lax.all_to_all(value, axes, 0, 0, tiled=True)


def summed_everywhere(value):
    plane = lax.axis_size(PLANE)
    column = lax.axis_size(COLUMN)
    chunks = value.reshape(plane, -1, LANES)
    part = jnp.sum(exchange(chunks, PLANE), axis=0)
    copies = jnp.broadcast_to(part[None], (column,) + part.shape)
    part = jnp.sum(exchange(copies, COLUMN), axis=0)
    copies = jnp.broadcast_to(part[None], (plane,) + part.shape)
    return exchange(copies, PLANE).reshape(value.shape)


def next_along(value, axis):
    count = lax.axis_size(axis)
    return lax.ppermute(value, axis, [(source, (source - 1) % count) for source in range(count)])


def iterate(states, energies, external, reorder):
    orbital = states[0]
    external = external.reshape(BLOCKS)
    order_blocks = reorder[0, 0].reshape(BLOCKS)
    column_index = lax.axis_index("x")

    cuts = (0, 1248, 1984, 2720, GRID)
    parts = [orbital[cuts[c] : cuts[c + 1]] for c in range(4)]
    count = lax.axis_size("zh")
    hops = [(4 * source, 4 * ((source - 1) % count)) for source in range(count)]
    hop0 = lax.ppermute(parts[0], KX, hops)
    spread = [lax.ppermute(parts[c], "x", [(0, c)]) for c in range(1, 4)]
    far_second = next_along(orbital, KY)
    beside = lax.ppermute(orbital, "x", [(1, 0), (2, 1), (3, 2)])
    inner = jnp.where(column_index == 1, spread[0], spread[1])
    outer, inner, own = lax.optimization_barrier((spread[2], inner, orbital))
    hop3 = lax.ppermute(outer, KX, [(s + 3, t + 3) for s, t in hops])
    hop12 = lax.ppermute(inner, KX, [(s + x, t + x) for s, t in hops for x in (1, 2)])
    second_energy = next_along(energies, KY)
    first_energy = next_along(energies, KX)

    turned, moved, potential, turned_late, moved_late = prepare(reorder[0, 0], own, order_blocks, external)
    potential, hop0, hop12 = lax.optimization_barrier((potential, hop0, hop12))
    pieces = [lax.ppermute(hop0, "x", [(0, 3)])]
    pieces += [lax.ppermute(hop12, "x", [(x, 3)]) for x in (1, 2)]
    second_states, second_terms = second_round_one(reorder[1, 0], far_second, turned, external, energies, second_energy)
    flag = (column_index == 3).astype(jnp.int32).reshape(1)
    first_states, terms = first_round_one(
        flag, pieces + [hop3], beside, moved, potential, order_blocks, energies, first_energy, second_terms
    )
    response, terms = round_two(
        summed_everywhere(terms), external, first_states, second_states, moved_late, turned_late, order_blocks,
        energies, first_energy, second_energy,
    )
    density = summed_everywhere(terms)
    return (response.reshape(1, NQ, 1, BANDS, BANDS), density.reshape(NQ, 1, GRID))


def solution(mesh):
    fine = Mesh(mesh.devices.reshape(AXIS_SIZES), AXES)
    return jax.shard_map(
        iterate,
        mesh=fine,
        in_specs=(
            P(AXES, None, None),
            P(AXES, None),
            P(),
            P(None, AXES, None),
        ),
        out_specs=(P(AXES, None, None, None, None), P()),
        check_vma=False,
    )
```

```python
import math

import jax
import jax.numpy as jnp
import numpy as np
from jax import lax
from jax.experimental import pallas as pl
from jax.experimental.pallas import tpu as pltpu
from jax.sharding import Mesh, PartitionSpec as P


AXES = ("zh", "x", "y", "zl", "core")
AXIS_SIZES = (4, 4, 4, 4, 2)
KX = ("zh", "x")
KY = ("y", "zl", "core")
PLANE = ("x", "y", "core")
COLUMN = ("zh", "zl")

GX = 64
GY = 64
NQ = 2
GRID = GX * GY
BANDS = 128
LANES = 128
ROWS = GRID // LANES
STEP = 512
LIMIT = 24 * 1024 * 1024

SMEAR = 0.5
FERMI = 0.0
SCREEN = 4.0


def hartley_table(length):
    positions = np.arange(length)
    angles = positions[:, None] * positions[None, :] % length * (2.0 * math.pi / length)
    return (np.cos(angles) + np.sin(angles)) / math.sqrt(length)


def screening(len_x, len_y):
    freq_x = np.arange(len_x)
    freq_x = np.minimum(freq_x, len_x - freq_x)
    freq_y = np.arange(len_y)
    freq_y = np.minimum(freq_y, len_y - freq_y)
    return 1.0 / (1.0 + (freq_x[:, None] ** 2 + freq_y[None, :] ** 2) / SCREEN)


def lane_block(index):
    return pl.ds(pl.multiple_of(index * LANES, LANES), LANES)


def in_parts(value):
    high = value.astype(jnp.bfloat16)
    rest = value - high.astype(jnp.float32)
    middle = rest.astype(jnp.bfloat16)
    low = (rest - middle.astype(jnp.float32)).astype(jnp.bfloat16)
    return (high, middle, low)


def occupation(energy):
    return 1.0 / (1.0 + jnp.exp((energy - FERMI) / SMEAR))


def across(row):
    return jnp.broadcast_to(row, (BANDS, BANDS)).T


def weights(energy, far_energy):
    energy = energy.astype(jnp.float32)
    far_energy = far_energy.astype(jnp.float32)
    gap = far_energy - across(energy)
    filled = across(occupation(energy)) - occupation(far_energy)
    return filled * gap / (gap * gap + SMEAR * SMEAR)


def weigh(potential_ref, own_ref, weighted_ref):
    for block in range(ROWS):
        at = slice(block * LANES, (block + 1) * LANES)
        product = potential_ref[block : block + 1, :] * own_ref[:, at].astype(jnp.float32)
        weighted_ref[:, at] = product.astype(jnp.bfloat16)


def respond(weighted_ref, far_ref, own_ref, weight, terms_ref):
    points = math.prod(AXIS_SIZES)
    bands = jnp.zeros((BANDS, BANDS), jnp.float32)
    for start in range(0, GRID, STEP):
        at = slice(start, start + STEP)
        bands += jnp.dot(weighted_ref[:, at], far_ref[at, :], preferred_element_type=jnp.float32)
    response = weight * (bands * (1.0 / math.sqrt(GRID)))
    low = response.astype(jnp.bfloat16)
    for start in range(0, GRID, STEP):
        at = slice(start, start + STEP)
        orbitals = lax.dot_general(
            low, far_ref[at, :], (((1,), (1,)), ((), ())), preferred_element_type=jnp.float32
        )
        term = jnp.sum(own_ref[:, at].astype(jnp.float32) * orbitals, axis=0, keepdims=True)
        term = term * (1.0 / math.sqrt(BANDS * points))
        for block in range(STEP // LANES):
            row = start // LANES + block
            terms_ref[row : row + 1, :] = term[:, block * LANES : (block + 1) * LANES]
    return response


def mark_columns(order_ref, column_ref):
    columns = lax.broadcasted_iota(jnp.int32, (LANES, LANES), 0)
    for block in range(ROWS):
        mine = (order_ref[block : block + 1, :] % LANES) == columns
        column_ref[:, block * LANES : (block + 1) * LANES] = jnp.where(mine, 1.0, 0.0).astype(jnp.bfloat16)


def to_far_order(value_ref, order_ref, column_ref, parts_ref):
    parts = in_parts(value_ref[...])
    rows = lax.broadcasted_iota(jnp.int32, (ROWS, LANES), 0)
    for block in range(ROWS):
        mine = (order_ref[block : block + 1, :] // LANES) == rows
        at = slice(block * LANES, (block + 1) * LANES)
        for index, part in enumerate(parts):
            wide = part[block : block + 1, :].astype(jnp.float32)
            parts_ref[index * ROWS : (index + 1) * ROWS, at] = jnp.where(mine, wide, 0.0).astype(jnp.bfloat16)
    sums = lax.dot_general(
        parts_ref[...], column_ref[...], (((1,), (1,)), ((), ())), preferred_element_type=jnp.float32
    )
    return sums[:ROWS] + sums[ROWS : 2 * ROWS] + sums[2 * ROWS :]


def from_far_order(value, order_ref, column_ref, out_ref, first_row):
    stacked = jnp.concatenate([part.astype(jnp.float32) for part in in_parts(value)]).astype(jnp.bfloat16)
    rows = lax.broadcasted_iota(jnp.int32, (ROWS, LANES), 0)
    for start in range(0, GRID, STEP):
        at = slice(start, start + STEP)
        spread = jnp.dot(stacked, column_ref[:, at], preferred_element_type=jnp.float32)
        spread = spread[:ROWS] + spread[ROWS : 2 * ROWS] + spread[2 * ROWS :]
        for block in range(STEP // LANES):
            row = start // LANES + block
            mine = (order_ref[row : row + 1, :] // LANES) == rows
            picked = jnp.where(mine, spread[:, block * LANES : (block + 1) * LANES], 0.0)
            out_ref[first_row + row : first_row + row + 1, :] = jnp.sum(picked, axis=0, keepdims=True)


UNROLL = 32


def started(sems, *pairs, first=0):
    copies = []
    for index, (source, target) in enumerate(pairs):
        copies.append(pltpu.make_async_copy(source, target, sems.at[first + index]))
        copies[-1].start()
    return copies


def finished(copies):
    for copy in copies:
        copy.wait()


def prepare_kernel(order_smem, own_ref, order_ref, external_ref,
                   turned_ref, moved_ref, potential_ref, turned_out, moved_out,
                   wide, scattered, parts, column, sems):
    wide[...] = own_ref[...].astype(jnp.float32)

    def move(step, carry):
        base = step * UNROLL
        for offset in range(UNROLL):
            row = base + offset
            scattered[pl.ds(order_smem[row], 1), :] = wide[pl.ds(row, 1), :]
        return carry

    lax.fori_loop(0, GRID // UNROLL, move, 0)

    def turn(block, carry):
        at = lane_block(block)
        turned_ref[:, at] = wide[at, :].T.astype(jnp.bfloat16)
        moved_ref[:, at] = scattered[at, :].T.astype(jnp.bfloat16)
        return carry

    lax.fori_loop(0, ROWS, turn, 0)
    copies = started(sems, (turned_ref, turned_out), (moved_ref, moved_out))
    mark_columns(order_ref, column)
    potential_ref[...] = to_far_order(external_ref, order_ref, column, parts)
    finished(copies)


def second_kernel(order_smem, sent_ref, turned_ref, external_ref, energy_ref, far_energy_ref,
                  far_out, terms_ref, wide, gathered, weighted, far_ref, sems):
    wide[...] = sent_ref[...].astype(jnp.float32)

    def move(step, carry):
        base = step * UNROLL
        for offset in range(UNROLL):
            row = base + offset
            gathered[pl.ds(row, 1), :] = wide[pl.ds(order_smem[row], 1), :]
        return carry

    lax.fori_loop(0, GRID // UNROLL, move, 0)
    far_ref[...] = gathered[...].astype(jnp.bfloat16)
    stores = started(sems, (far_ref, far_out))
    weigh(external_ref, turned_ref, weighted)
    respond(weighted, far_ref, turned_ref, weights(energy_ref[...], far_energy_ref[...]), terms_ref)
    finished(stores)


def first_kernel(flag_smem, *refs):
    piece_refs = refs[:4]
    (beside_ref, moved_ref, potential_ref, order_ref, energy_ref, far_energy_ref, other_ref,
     far_out, terms_ref, own_terms, far_ref, weighted_ref, column_ref, sems) = refs[4:]

    @pl.when(flag_smem[0] == 1)
    def _():
        last = piece_refs[3]
        start = GRID - last.shape[0]
        copies = started(sems, (last, far_ref.at[pl.ds(start, last.shape[0])]), first=1)
        start = 0
        for piece in piece_refs[:3]:
            far_ref[start : start + piece.shape[0], :] = piece[...]
            start += piece.shape[0]
        finished(copies)

    @pl.when(flag_smem[0] == 0)
    def _():
        far_ref[...] = beside_ref[...]

    stores = started(sems, (far_ref, far_out))
    weight = weights(energy_ref[...], far_energy_ref[...])
    weigh(potential_ref, moved_ref, weighted_ref)
    mark_columns(order_ref, column_ref)
    respond(weighted_ref, far_ref, moved_ref, weight, own_terms)
    from_far_order(own_terms[...], order_ref, column_ref, terms_ref, 0)
    terms_ref[ROWS:, :] = other_ref[...]
    finished(stores)


def exact_dot(left, right):
    return jnp.dot(left, right, precision=lax.Precision.HIGHEST, preferred_element_type=jnp.float32)


def last_kernel(density_ref, external_ref, even_ref, odd_ref, into_ref, back_ref, screen_ref, even_t_ref, odd_t_ref,
                first_in, second_in, moved_in, turned_in, order_ref,
                energy_ref, first_energy_ref, second_energy_ref,
                response_ref, terms_ref, parts, potential, moved_potential, weighted, own_terms,
                first_ref, second_ref, moved_ref, turned_ref, column_ref, sems):
    loads = started(sems, (moved_in, moved_ref), (first_in, first_ref))
    later = started(sems, (turned_in, turned_ref), (second_in, second_ref), first=2)
    mark_columns(order_ref, column_ref)
    low_half = lax.broadcasted_iota(jnp.int32, (ROWS, LANES), 1) < GY
    along_y = exact_dot(density_ref[...], into_ref[...])
    for q_index in range(NQ):
        at = slice(q_index * ROWS, (q_index + 1) * ROWS)
        spectrum = exact_dot(even_ref[...], along_y[at, :LANES]) + exact_dot(odd_ref[...], along_y[at, LANES:])
        back = exact_dot(spectrum * screen_ref[...], back_ref[...])
        field = jnp.where(low_half, exact_dot(even_t_ref[...], back), exact_dot(odd_t_ref[...], back))
        potential[at, :] = external_ref[...] + field
    moved_potential[...] = to_far_order(potential.at[0:ROWS], order_ref, column_ref, parts)
    finished(loads)
    weigh(moved_potential, moved_ref, weighted)
    weight = weights(energy_ref[...], first_energy_ref[...])
    response_ref[0] = respond(weighted, first_ref, moved_ref, weight, own_terms).T
    from_far_order(own_terms[...], order_ref, column_ref, terms_ref, 0)
    finished(later)
    weigh(potential.at[ROWS : 2 * ROWS], turned_ref, weighted)
    weight = weights(energy_ref[...], second_energy_ref[...])
    response_ref[1] = respond(weighted, second_ref, turned_ref, weight, own_terms).T
    terms_ref[ROWS:, :] = own_terms[...]


def coulomb_tables():
    table = hartley_table(GX)
    other = hartley_table(GY)
    none = np.zeros((GY, 2 * GY))
    twice = np.concatenate([other, other], axis=1)
    into = np.concatenate([np.concatenate([twice, none]), np.concatenate([none, twice])], axis=1)
    back = np.concatenate([twice, none])
    screen = screening(GX, GY)
    screen = np.concatenate([screen, screen], axis=1)
    even, odd = table[:, 0::2], table[:, 1::2]
    return [part.astype(np.float32) for part in (even, odd, into, back, screen, even.T, odd.T)]


VMEM = pl.BlockSpec(memory_space=pltpu.VMEM)
SMEM = pl.BlockSpec(memory_space=pltpu.SMEM)
HBM = pl.BlockSpec(memory_space=pltpu.HBM)
KEPT = pl.BlockSpec(memory_space=pltpu.VMEM)
PLACES = {id(HBM): pltpu.HBM, id(KEPT): pltpu.VMEM}


def local_call(kernel, arrays, in_specs, outs, scratch, copies, microseconds, limit=None):
    return pl.pallas_call(
        kernel,
        out_shape=[
            PLACES.get(id(spec), jax.ShapeDtypeStruct)(shape, kind) for shape, kind, spec in outs
        ],
        in_specs=in_specs,
        out_specs=[spec for shape, kind, spec in outs],
        scratch_shapes=[pltpu.VMEM(shape, kind) for shape, kind in scratch] + [pltpu.SemaphoreType.DMA((copies,))],
        cost_estimate=pl.CostEstimate(flops=0, bytes_accessed=microseconds * 3000000, transcendentals=0),
        compiler_params=pltpu.CompilerParams(vmem_limit_bytes=limit),
    )(*arrays)


F32 = jnp.float32
BF16 = jnp.bfloat16
TALL = (GRID, BANDS)
TURNED = (BANDS, GRID)
BLOCKS = (ROWS, LANES)


def prepare(order, own, order_blocks, external):
    return local_call(
        prepare_kernel, (order, own, order_blocks, external), [SMEM, VMEM, VMEM, VMEM],
        [(TURNED, BF16, KEPT)] * 2 + [(BLOCKS, F32, VMEM)] + [(TURNED, BF16, HBM)] * 2,
        [(TALL, F32), (TALL, F32), ((3 * ROWS, GRID), BF16), (TURNED, BF16)], 2, 10,
        LIMIT,
    )


def second_round_one(order, sent, turned, external, energy, far_energy):
    sent = pltpu.with_memory_space_constraint(sent, pltpu.VMEM)
    turned = pltpu.with_memory_space_constraint(turned, pltpu.VMEM)
    return local_call(
        second_kernel, (order, sent, turned, external, energy, far_energy),
        [SMEM, VMEM, VMEM, VMEM, VMEM, VMEM],
        [(TALL, BF16, HBM), (BLOCKS, F32, VMEM)],
        [(TALL, F32), (TALL, F32), (TURNED, BF16), (TALL, BF16)], 1, 7, LIMIT,
    )


def first_round_one(flag, pieces, beside, moved, potential, order_blocks, energy, far_energy, other):
    places = [pltpu.VMEM] * 3 + [pltpu.HBM]
    pieces = [pltpu.with_memory_space_constraint(piece, place) for piece, place in zip(pieces, places)]
    beside = pltpu.with_memory_space_constraint(beside, pltpu.VMEM)
    moved = pltpu.with_memory_space_constraint(moved, pltpu.VMEM)
    return local_call(
        first_kernel, (flag, *pieces, beside, moved, potential, order_blocks, energy, far_energy, other),
        [SMEM] + [VMEM] * 3 + [HBM] + [VMEM] * 7,
        [(TALL, BF16, HBM), ((2 * ROWS, LANES), F32, VMEM)],
        [(BLOCKS, F32), (TALL, BF16), (TURNED, BF16), (TURNED, BF16)], 2, 3, LIMIT,
    )


def round_two(density, external, first, second, moved, turned, order_blocks, energy, first_energy, second_energy):
    arrays = (density, external, *[jnp.asarray(part) for part in coulomb_tables()], first, second, moved, turned,
              order_blocks, energy, first_energy, second_energy)
    return local_call(
        last_kernel, arrays, [VMEM] * 9 + [HBM] * 4 + [VMEM] * 4,
        [((NQ, BANDS, BANDS), F32, VMEM), ((2 * ROWS, LANES), F32, VMEM)],
        [((3 * ROWS, GRID), BF16), ((2 * ROWS, LANES), F32), (BLOCKS, F32), (TURNED, BF16), (BLOCKS, F32)]
        + [(TALL, BF16)] * 2 + [(TURNED, BF16)] * 3, 4, 5,
    )


def exchange(value, axes):
    return lax.all_to_all(value, axes, 0, 0, tiled=True)


def summed_everywhere(value):
    plane = lax.axis_size(PLANE)
    column = lax.axis_size(COLUMN)
    chunks = value.reshape(plane, -1, LANES)
    part = jnp.sum(exchange(chunks, PLANE), axis=0)
    copies = jnp.broadcast_to(part[None], (column,) + part.shape)
    part = jnp.sum(exchange(copies, COLUMN), axis=0)
    copies = jnp.broadcast_to(part[None], (plane,) + part.shape)
    return exchange(copies, PLANE).reshape(value.shape)


def next_along(value, axis):
    count = lax.axis_size(axis)
    return lax.ppermute(value, axis, [(source, (source - 1) % count) for source in range(count)])


def iterate(states, energies, external, reorder):
    orbital = states[0]
    external = external.reshape(BLOCKS)
    order_blocks = reorder[0, 0].reshape(BLOCKS)
    column_index = lax.axis_index("x")

    cuts = (0, 1152, 1856, 2560, GRID)
    parts = [orbital[cuts[c] : cuts[c + 1]] for c in range(4)]
    count = lax.axis_size("zh")
    hops = [(4 * source, 4 * ((source - 1) % count)) for source in range(count)]
    hop0 = lax.ppermute(parts[0], KX, hops)
    spread = [lax.ppermute(parts[c], "x", [(0, c)]) for c in range(1, 4)]
    far_second = next_along(orbital, KY)
    beside = lax.ppermute(orbital, "x", [(1, 0), (2, 1), (3, 2)])
    inner = jnp.where(column_index == 1, spread[0], spread[1])
    hop3 = lax.ppermute(spread[2], KX, [(s + 3, t + 3) for s, t in hops])
    hop12 = lax.ppermute(inner, KX, [(s + x, t + x) for s, t in hops for x in (1, 2)])
    second_energy = next_along(energies, KY)
    first_energy = next_along(energies, KX)

    turned, moved, potential, turned_late, moved_late = prepare(reorder[0, 0], orbital, order_blocks, external)
    second_states, second_terms = second_round_one(reorder[1, 0], far_second, turned, external, energies, second_energy)
    second_terms, hop0, hop12 = lax.optimization_barrier((second_terms, hop0, hop12))
    pieces = [lax.ppermute(hop0, "x", [(0, 3)])]
    pieces += [lax.ppermute(hop12, "x", [(x, 3)]) for x in (1, 2)]
    flag = (column_index == 3).astype(jnp.int32).reshape(1)
    first_states, terms = first_round_one(
        flag, pieces + [hop3], beside, moved, potential, order_blocks, energies, first_energy, second_terms
    )
    response, terms = round_two(
        summed_everywhere(terms), external, first_states, second_states, moved_late, turned_late, order_blocks,
        energies, first_energy, second_energy,
    )
    density = summed_everywhere(terms)
    return (response.reshape(1, NQ, 1, BANDS, BANDS), density.reshape(NQ, 1, GRID))


def solution(mesh):
    fine = Mesh(mesh.devices.reshape(AXIS_SIZES), AXES)
    return jax.shard_map(
        iterate,
        mesh=fine,
        in_specs=(
            P(AXES, None, None),
            P(AXES, None),
            P(),
            P(None, AXES, None),
        ),
        out_specs=(P(AXES, None, None, None, None), P()),
        check_vma=False,
    )
```
